128 devices in a mesh: views: 8 (over z, core), bricks: 16 (over y, x).
Axes of the slice: x: 4, y: 4, z: 4, core: 2. Of those that a mesh axis runs over, the one named last changes fastest.
Arguments:
- tile_pixel: int32 [8, 16, 128], P('views', 'bricks'), may hold values from 0 to 15
- tile_voxel: int32 [8, 16, 128], P('views', 'bricks'), may hold values from 0 to 63
- tile_count: int32 [8, 16], P('views', 'bricks'), may hold values from 32 to 128, as said below
- features: bfloat16 [8, 16, 16, 64, 128], P('views', 'bricks'), may hold values from -6 to 6
- interp: bfloat16 [8, 16, 128, 128, 512], P('views', 'bricks'), may hold values from -0.5 to 0.5
- conv_weight: bfloat16 [3, 3, 3, 64, 64], replicated, may hold values from -0.15625 to 0.15625
- conv_bias: float32 [64], replicated, may hold values from -3 to 3
- smooth_coef: float32 [128, 256, 128], P('bricks', 'views'), may hold values from 0.04 to 0.16
Outputs:
- volume: bfloat16 [64, 128, 256, 128], P(None, 'bricks', 'views')
The draws below stay inside these ranges and needn't reach their ends.
Inputs may be any that keep to these rules, and one draw needn't show every extreme that they name: `tile_count`: between 32 and 128 live tiles a device; counts are shared largely within a view group; some device has all 128 slots live in every draw.
All inputs are finite; a program needn't handle non-finite values.
Results may differ from the reference program's by a relative error of at most 0.0037.
Values may be sent and summed in bfloat16 or wider, within the bound.
No kernel may reach another device: no remote copies, remote signals or barrier semaphores. Data moves between devices by JAX's collectives and lax.ppermute only.
A program may use at most 256 MiB of HBM per device.

```python
import math
import jax
import jax.numpy as jnp
from jax import lax

C = 64
PIX = 128
Z = 128
BX = 8
BY = 32
PIXB = 16
BLK_DEV = 64
VOXB = 512
X = 128
Y = 256
N_VIEWS = 8
N_BRICKS = 16
DEVICES = 128


def draw_tile_count(key, part):
    key_top = jax.random.fold_in(key, 11)
    key_drop = jax.random.fold_in(key, 12)
    key_pick = jax.random.fold_in(key, 13)
    lowest = DEVICES // 4
    view_top = jax.random.randint(key_top, (N_VIEWS, 1), lowest, DEVICES + 1)
    dropped = jax.random.randint(key_drop, (N_VIEWS, N_BRICKS), 0, DEVICES // 4 + 1)
    counts = jnp.maximum(view_top - dropped, lowest).reshape(-1)
    picked = jax.random.randint(key_pick, (), 0, N_VIEWS * N_BRICKS)
    counts = jnp.where(jnp.arange(N_VIEWS * N_BRICKS) == picked, DEVICES, counts)
    return counts.reshape(N_VIEWS, N_BRICKS).astype(jnp.int32)


def with_ends(array, rng, smallest, top_value):
    dims = array.shape
    spot = [jax.random.randint(jax.random.fold_in(rng, axis), (), 0, dims[axis]) for axis in range(len(dims))]
    array = array.at[tuple(spot)].set(smallest)
    longest = dims.index(max(dims))
    spot[longest] = (spot[longest] + 1) % dims[longest]
    return array.at[tuple(spot)].set(top_value)


def levels(rng, shape, cuts, low, top_value):
    gain, own = 1.0, jax.random.fold_in(rng, 6)
    for axis_at, shards_of in cuts:
        draws = jnp.exp(jax.random.uniform(jax.random.fold_in(own, axis_at), (shards_of,), jnp.float32, low / len(cuts), top_value / len(cuts)))
        gain = gain * jnp.repeat(draws, shape[axis_at] // shards_of).reshape([-1 if axis == axis_at else 1 for axis in range(len(shape))])
    return gain


def scatter_about(stream_key, dims, scale, most, cuts=(), kind=jnp.bfloat16):
    gain = levels(stream_key, dims, cuts, -0.22, 0.18) if cuts else 1.0
    values = jax.random.normal(stream_key, dims, jnp.float32) * scale * gain
    return jnp.minimum(jnp.maximum(values, -most), most).astype(kind)


def setup_inputs(seed: int = 0) -> dict:
    seeds = jax.random.split(jax.random.key(seed), 9)
    return {
        "tile_pixel": with_ends(jax.random.randint(seeds[0], (N_VIEWS, N_BRICKS, N_VIEWS * N_BRICKS), 0, PIXB), jax.random.fold_in(seeds[0], 1), 0, PIXB - 1).astype(jnp.int32),
        "tile_voxel": with_ends(jax.random.randint(seeds[1], (N_VIEWS, N_BRICKS, N_VIEWS * N_BRICKS), 0, BLK_DEV), jax.random.fold_in(seeds[1], 1), 0, BLK_DEV - 1).astype(jnp.int32),
        "tile_count": draw_tile_count(jax.random.fold_in(seeds[8], 71), 0),
        "features": scatter_about(seeds[3], (N_VIEWS, N_BRICKS, PIXB, C, PIX), 1.0, 6.0, ((0, 8), (1, 16))),
        "interp": scatter_about(seeds[4], (N_VIEWS, N_BRICKS, N_VIEWS * N_BRICKS, PIX, VOXB), PIX ** -0.5, 0.5, ((0, 8), (1, 16))),
        "conv_weight": scatter_about(seeds[5], (3, 3, 3, C, C), (27 * C) ** -0.5, 0.15625),
        "conv_bias": scatter_about(seeds[6], (C,), 0.5, 3.0, (), jnp.float32),
        "smooth_coef": jnp.clip(jnp.exp(math.log(0.16) - 1.3862944 * jax.random.uniform(seeds[7], (X, Y, Z), jnp.float32) ** levels(seeds[7], (X, Y, Z), ((0, 16), (1, 8)), -0.2, 0.2)), 0.04, 0.16),
    }


def lift_step(total, item):
    feats, tiles, pixel_ids, voxel_ids, count, sender = item
    slot_ids = jnp.arange(DEVICES, dtype=jnp.int32)
    offset = jnp.remainder(sender * 37, DEVICES)
    live = (jnp.remainder(slot_ids - offset, DEVICES) < count).astype(jnp.float32)
    chosen = feats[pixel_ids]
    part = jnp.einsum("dcp,dpv->dcv", chosen.astype(jnp.float32), tiles.astype(jnp.float32))
    rounded = lax.optimization_barrier(part.astype(jnp.bfloat16))
    part = rounded.astype(jnp.float32)
    total = total.at[slot_ids, voxel_ids].add(part * live[:, None, None])
    return total, None


def convolve_slab(stacked, weights, conv_bias, width_x, width_y):
    total = jnp.zeros((C, width_x, width_y, Z), jnp.float32)
    for shift_x in range(3):
        for shift_y in range(3):
            window = stacked[:, shift_x:shift_x + width_x, shift_y:shift_y + width_y, :]
            total = total + jnp.einsum("oi,ixyz->oxyz", weights[shift_x * 3 + shift_y].astype(jnp.float32), window.astype(jnp.float32))
    return jax.nn.relu(total + conv_bias[:, None, None, None])


def reference(tile_pixel, tile_voxel, tile_count, features, interp, conv_weight, conv_bias, smooth_coef):
    senders = jnp.arange(DEVICES, dtype=jnp.int32)
    items = (features.reshape(DEVICES, PIXB, C, PIX), interp.reshape(DEVICES, DEVICES, PIX, VOXB),
             tile_pixel.reshape(DEVICES, DEVICES), tile_voxel.reshape(DEVICES, DEVICES),
             tile_count.reshape(DEVICES), senders)
    start = jnp.zeros((DEVICES, BLK_DEV, C, VOXB), jnp.float32)
    blocks, unused = lax.scan(lift_step, start, items)
    blocks = blocks.reshape(N_VIEWS, N_BRICKS, BX, BY // 4, C, 4, Z)
    lifted = jnp.transpose(blocks, (4, 1, 2, 0, 3, 5, 6)).reshape(C, X, Y, Z)
    rectified = jax.nn.relu(lifted).astype(jnp.bfloat16)
    padded = jnp.pad(rectified, ((0, 0), (1, 1), (1, 1), (1, 1)))
    stacked = jnp.concatenate([padded[..., 0:Z], padded[..., 1:Z + 1], padded[..., 2:Z + 2]], axis=0)
    weights = jnp.transpose(conv_weight, (0, 1, 3, 2, 4)).reshape(9, C, 3 * C)

    def slab(index):
        piece = lax.dynamic_slice_in_dim(stacked, index * BX, BX + 2, 1)
        return convolve_slab(piece, weights, conv_bias, BX, Y)

    slabs = lax.map(slab, jnp.arange(N_BRICKS, dtype=jnp.int32))
    gated = jnp.transpose(slabs, (1, 0, 2, 3, 4)).reshape(C, X, Y, Z)
    beside_all = jnp.pad(gated, ((0, 0), (1, 1), (1, 1), (1, 1)))
    beside = beside_all[:, 2:, 1:-1, 1:-1] + beside_all[:, :-2, 1:-1, 1:-1]
    beside = beside + beside_all[:, 1:-1, 2:, 1:-1] + beside_all[:, 1:-1, :-2, 1:-1]
    beside = beside + beside_all[:, 1:-1, 1:-1, 2:] + beside_all[:, 1:-1, 1:-1, :-2]
    volume = gated + smooth_coef[None] * (beside - 6.0 * gated)
    return volume.astype(jnp.bfloat16)
```

```python
import functools

import jax
import jax.numpy as jnp
from jax import lax
from jax.experimental import pallas as pl
from jax.experimental.pallas import tpu as pltpu
from jax.sharding import PartitionSpec as P

C = 64
PIX = 128
Z = 128
BX = 8
BY = 32
BLK = 64
VOXB = 512
ROW = BY * Z
WIDE = (BY + 4) * Z
GATED = (BY + 2) * Z
SEND = 8


def lift_kernel(tgt_ref, part_ref, main_ref, lo_ref, hi_ref, ylo_ref, yhi_ref, acc):
    step = pl.program_id(0)

    @pl.when(step == 0)
    def _():
        acc[...] = jnp.zeros_like(acc)

    for i in range(SEND):
        block = tgt_ref[step * SEND + i]

        @pl.when(block < BLK)
        def _():
            acc[block] = acc[block] + part_ref[i].astype(jnp.float32)

    @pl.when(step == pl.num_programs(0) - 1)
    def _():
        def plane(x, carry):
            for yb in range(BY // 4):
                v = jnp.maximum(acc[x * (BY // 4) + yb], 0.0).astype(jnp.bfloat16)
                main_ref[x, :, yb * VOXB : (yb + 1) * VOXB] = v
                if yb == 0:
                    ylo_ref[x] = v[:, : 2 * Z]
                if yb == BY // 4 - 1:
                    yhi_ref[x] = v[:, 2 * Z :]
            return carry

        lax.fori_loop(0, BX, plane, 0)
        lo_ref[...] = main_ref[0:2]
        hi_ref[...] = main_ref[BX - 2 : BX]


def lift(tgt, part):
    n = part.shape[0]
    whole = lambda *shape: pl.BlockSpec(shape, lambda i, t: (0,) * len(shape))
    return pl.pallas_call(
        lift_kernel,
        grid_spec=pltpu.PrefetchScalarGridSpec(
            num_scalar_prefetch=1,
            grid=(n // SEND,),
            in_specs=[pl.BlockSpec((SEND, C, VOXB), lambda i, t: (i, 0, 0))],
            out_specs=[
                whole(BX, C, ROW),
                whole(2, C, ROW),
                whole(2, C, ROW),
                whole(BX, C, 2 * Z),
                whole(BX, C, 2 * Z),
            ],
            scratch_shapes=[pltpu.VMEM((BLK, C, VOXB), jnp.float32)],
        ),
        out_shape=[
            jax.ShapeDtypeStruct((BX, C, ROW), jnp.bfloat16),
            jax.ShapeDtypeStruct((2, C, ROW), jnp.bfloat16),
            jax.ShapeDtypeStruct((2, C, ROW), jnp.bfloat16),
            jax.ShapeDtypeStruct((BX, C, 2 * Z), jnp.bfloat16),
            jax.ShapeDtypeStruct((BX, C, 2 * Z), jnp.bfloat16),
        ],
        compiler_params=pltpu.CompilerParams(vmem_limit_bytes=48 << 20),
        name="lift",
    )(tgt, part)


def conv_kernel(
    flags_ref,
    w_ref,
    bias_ref,
    coef_ref,
    main_ref,
    xlo_ref,
    xhi_ref,
    ylo_ref,
    yhi_ref,
    clo_ref,
    chi_ref,
    out_ref,
    xs,
    acc_a,
    acc_b,
    gated,
    flat,
):
    step = pl.program_id(0)
    lane = lax.broadcasted_iota(jnp.int32, (C, Z), 1)
    first = lane == 0
    last = lane == Z - 1

    def stage(pieces):
        at = 0
        for ref, count in pieces:
            for y in range(count):
                v = ref[:, y * Z : (y + 1) * Z]
                f = v.astype(jnp.float32)
                below = jnp.where(first, 0.0, pltpu.roll(f, 1, 1)).astype(jnp.bfloat16)
                above = jnp.where(last, 0.0, pltpu.roll(f, Z - 1, 1)).astype(jnp.bfloat16)
                xs[0:C, at * Z : (at + 1) * Z] = below
                xs[C : 2 * C, at * Z : (at + 1) * Z] = v
                xs[2 * C : 3 * C, at * Z : (at + 1) * Z] = above
                at += 1

    @pl.when(step < 2)
    def _():
        stage([(clo_ref.at[0, 0], 2), (xlo_ref.at[0], BY), (clo_ref.at[1, 0], 2)])

    @pl.when((step >= 2) & (step < BX + 2))
    def _():
        stage([(ylo_ref.at[0], 2), (main_ref.at[0], BY), (yhi_ref.at[0], 2)])

    @pl.when(step >= BX + 2)
    def _():
        stage([(chi_ref.at[0, 0], 2), (xhi_ref.at[0], BY), (chi_ref.at[1, 0], 2)])

    slot = lax.rem(step, 3)
    keep = jnp.where(step == 2, flags_ref[0], jnp.where(step == BX + 3, flags_ref[1], 1.0))
    bias = jnp.broadcast_to(bias_ref[...], (C, 2 * Z))
    weights = w_ref[...]
    for t in range((BY + 2) // 2):
        cols = slice(t * 2 * Z, (t + 1) * 2 * Z)
        window = jnp.concatenate(
            [xs[:, (t * 2 + dy) * Z : (t * 2 + dy + 2) * Z] for dy in range(3)], axis=0
        )
        p = jnp.dot(weights, window, preferred_element_type=jnp.float32)
        done = acc_b[:, cols] + p[2 * C : 3 * C]
        g = jnp.maximum(done + bias, 0.0) * keep
        if t == 0:
            gated[slot, :, 0:Z] = g[:, :Z] * flags_ref[2]
            gated[slot, :, Z : 2 * Z] = g[:, Z:]
        elif t == BY // 2:
            gated[slot, :, BY * Z : (BY + 1) * Z] = g[:, :Z]
            gated[slot, :, (BY + 1) * Z : (BY + 2) * Z] = g[:, Z:] * flags_ref[3]
        else:
            gated[slot, :, cols] = g
        acc_b[:, cols] = acc_a[:, cols] + p[C : 2 * C]
        acc_a[:, cols] = p[0:C]

    @pl.when(step >= 4)
    def _():
        mid = lax.rem(step + 2, 3)
        old = lax.rem(step + 1, 3)
        for y in range(BY):
            here = slice((y + 1) * Z, (y + 2) * Z)
            g = gated[mid, :, here]
            beside = gated[slot, :, here] + gated[old, :, here]
            beside = beside + gated[mid, :, y * Z : (y + 1) * Z]
            beside = beside + gated[mid, :, (y + 2) * Z : (y + 3) * Z]
            beside = beside + jnp.where(first, 0.0, pltpu.roll(g, 1, 1))
            beside = beside + jnp.where(last, 0.0, pltpu.roll(g, Z - 1, 1))
            coef = jnp.broadcast_to(coef_ref[0, y : y + 1, :], (C, Z))
            flat[pl.ds(y, C, stride=BY), :] = g + coef * (beside - 6.0 * g)
        out_ref[:, 0] = flat[...].reshape(C, BY, Z).astype(jnp.bfloat16)


def conv_smooth(flags, weights, bias, coef, main, xlo, xhi, ylo, yhi, clo, chi):
    local = lambda i, f: (jnp.clip(i - 2, 0, BX - 1), 0, 0)
    low = lambda i, f: (jnp.minimum(i, 1), 0, 0)
    high = lambda i, f: (jnp.clip(i - BX - 2, 0, 1), 0, 0)
    done = lambda i: jnp.clip(i - 4, 0, BX - 1)
    return pl.pallas_call(
        conv_kernel,
        grid_spec=pltpu.PrefetchScalarGridSpec(
            num_scalar_prefetch=1,
            grid=(BX + 4,),
            in_specs=[
                pl.BlockSpec((3 * C, 9 * C), lambda i, f: (0, 0)),
                pl.BlockSpec((C, 1), lambda i, f: (0, 0)),
                pl.BlockSpec((1, BY, Z), lambda i, f: (done(i), 0, 0)),
                pl.BlockSpec((1, C, ROW), local),
                pl.BlockSpec((1, C, ROW), low),
                pl.BlockSpec((1, C, ROW), high),
                pl.BlockSpec((1, C, 2 * Z), local),
                pl.BlockSpec((1, C, 2 * Z), local),
                pl.BlockSpec((2, 1, C, 2 * Z), lambda i, f: (0, jnp.minimum(i, 1), 0, 0)),
                pl.BlockSpec((2, 1, C, 2 * Z), lambda i, f: (0, jnp.clip(i - BX - 2, 0, 1), 0, 0)),
            ],
            out_specs=pl.BlockSpec((C, 1, BY, Z), lambda i, f: (0, done(i), 0, 0)),
            scratch_shapes=[
                pltpu.VMEM((3 * C, WIDE), jnp.bfloat16),
                pltpu.VMEM((C, GATED), jnp.float32),
                pltpu.VMEM((C, GATED), jnp.float32),
                pltpu.VMEM((3, C, GATED), jnp.float32),
                pltpu.VMEM((C * BY, Z), jnp.float32),
            ],
        ),
        out_shape=jax.ShapeDtypeStruct((C, BX, BY, Z), jnp.bfloat16),
        compiler_params=pltpu.CompilerParams(vmem_limit_bytes=48 << 20),
        name="conv_smooth",
    )(flags, weights, bias, coef, main, xlo, xhi, ylo, yhi, clo, chi)


def shift(array, axis, by):
    size = lax.axis_size(axis)
    pairs = [(i, i + by) for i in range(size) if 0 <= i + by < size]
    return lax.ppermute(array, axis, pairs)


def on_device(
    tile_pixel, tile_voxel, tile_count, features, interp, conv_weight, conv_bias, smooth_coef
):
    feats = features[0, 0]
    tiles = interp[0, 0]
    pixel_ids = tile_pixel[0, 0]
    voxel_ids = tile_voxel[0, 0]
    count = tile_count[0, 0]
    slots_total = tiles.shape[0]
    n_bricks = lax.axis_size("bricks")
    n_views = lax.axis_size("views")
    brick = lax.axis_index("bricks")
    view = lax.axis_index("views")
    me = view * n_bricks + brick
    slot_ids = jnp.arange(slots_total, dtype=jnp.int32)
    live = jnp.remainder(slot_ids - jnp.remainder(me * 37, slots_total), slots_total) < count
    targets = lax.all_gather(
        jnp.where(live, voxel_ids, BLK), ("views", "bricks"), axis=0, tiled=False
    )
    tgt = lax.dynamic_slice_in_dim(targets.reshape(slots_total, slots_total), me, 1, axis=1)[:, 0]
    selector = (pixel_ids[:, None] == jnp.arange(feats.shape[0], dtype=jnp.int32)[None, :]).astype(
        jnp.bfloat16
    )
    chosen = jnp.einsum(
        "dk,kq->dq", selector, feats.reshape(feats.shape[0], C * PIX),
        preferred_element_type=jnp.float32,
    )
    chosen = chosen.astype(jnp.bfloat16).reshape(slots_total, C, PIX)
    partial_value = jnp.einsum(
        "dcp,dpv->dcv", chosen, tiles, preferred_element_type=jnp.float32
    ).astype(jnp.bfloat16)
    got = lax.all_to_all(partial_value, ("views", "bricks"), split_axis=0, concat_axis=0, tiled=True)
    main, lo, hi, ylo, yhi = lift(tgt, got)
    from_low = shift(yhi, "views", 1)
    from_high = shift(ylo, "views", -1)
    xlo = shift(hi, "bricks", 1)
    xhi = shift(lo, "bricks", -1)
    clo = shift(jnp.stack([from_low[BX - 2 :], from_high[BX - 2 :]]), "bricks", 1)
    chi = shift(jnp.stack([from_low[:2], from_high[:2]]), "bricks", -1)
    flags = jnp.stack(
        [brick > 0, brick < n_bricks - 1, view > 0, view < n_views - 1]
    ).astype(jnp.float32)
    weights = jnp.transpose(conv_weight, (0, 3, 1, 2, 4)).reshape(3 * C, 9 * C)
    return conv_smooth(
        flags, weights, conv_bias[:, None], smooth_coef, main, xlo, xhi, from_low, from_high, clo, chi
    )


def solution(mesh):
    in_specs = (
        P("views", "bricks", None),
        P("views", "bricks", None),
        P("views", "bricks"),
        P("views", "bricks", None, None, None),
        P("views", "bricks", None, None, None),
        P(),
        P(),
        P("bricks", "views", None),
    )
    out_specs = P(None, "bricks", "views", None)
    return jax.shard_map(
        on_device, mesh=mesh, in_specs=in_specs, out_specs=out_specs, check_vma=False
    )
```

```python
import functools

import jax
import jax.numpy as jnp
from jax import lax
from jax.experimental import pallas as pl
from jax.experimental.pallas import tpu as pltpu
from jax.sharding import PartitionSpec as P

C = 64
PIX = 128
Z = 128
BX = 8
BY = 32
BLK = 64
VOXB = 512
ROW = BY * Z
WIDE = (BY + 4) * Z
GATED = (BY + 2) * Z
SEND = 16
PITCH = 40


def lift_kernel(tgt_ref, part_ref, main_ref, lo_ref, hi_ref, ylo_ref, yhi_ref, part, acc, sems):
    chunks = part.shape[0] // SEND
    copies = []
    for k in range(chunks):
        rows = pl.ds(k * SEND, SEND)
        copies.append(pltpu.make_async_copy(part_ref.at[rows], part.at[rows], sems.at[k]))
        copies[-1].start()
    acc[...] = jnp.zeros_like(acc)
    for k in range(chunks):
        copies[k].wait()

        def add(i, carry):
            block = tgt_ref[i]
            acc[block] = acc[block] + part[i].astype(jnp.float32)
            return carry

        lax.fori_loop(k * SEND, (k + 1) * SEND, add, 0)

    def plane(x, carry):
        for yb in range(BY // 4):
            v = jnp.maximum(acc[x * (BY // 4) + yb], 0.0).astype(jnp.bfloat16)
            main_ref[x, :, yb * VOXB : (yb + 1) * VOXB] = v
            if yb == 0:
                ylo_ref[x] = v[:, : 2 * Z]
            if yb == BY // 4 - 1:
                yhi_ref[x] = v[:, 2 * Z :]
        return carry

    lax.fori_loop(0, BX, plane, 0)
    lo_ref[...] = main_ref[0:2]
    hi_ref[...] = main_ref[BX - 2 : BX]


def lift(tgt, part):
    n = part.shape[0]
    vmem = pl.BlockSpec(memory_space=pltpu.VMEM)
    return pl.pallas_call(
        lift_kernel,
        in_specs=[pl.BlockSpec(memory_space=pltpu.SMEM), pl.BlockSpec(memory_space=pl.ANY)],
        out_specs=[vmem] * 5,
        scratch_shapes=[
            pltpu.VMEM((n, C, VOXB), jnp.bfloat16),
            pltpu.VMEM((BLK + 1, C, VOXB), jnp.float32),
            pltpu.SemaphoreType.DMA((n // SEND,)),
        ],
        out_shape=[
            jax.ShapeDtypeStruct((BX, C, ROW), jnp.bfloat16),
            jax.ShapeDtypeStruct((2, C, ROW), jnp.bfloat16),
            jax.ShapeDtypeStruct((2, C, ROW), jnp.bfloat16),
            jax.ShapeDtypeStruct((BX, C, 2 * Z), jnp.bfloat16),
            jax.ShapeDtypeStruct((BX, C, 2 * Z), jnp.bfloat16),
        ],
        compiler_params=pltpu.CompilerParams(vmem_limit_bytes=48 << 20),
        name="lift",
    )(tgt, part)


def conv_kernel(
    flags_ref,
    w_ref,
    bias_ref,
    coef_ref,
    main_ref,
    xlo_ref,
    xhi_ref,
    ylo_ref,
    yhi_ref,
    clo_ref,
    chi_ref,
    out_ref,
    raw,
    xs_a,
    xs_b,
    acc_a,
    acc_b,
    prev,
    pend,
    flat_a,
    flat_b,
    sems,
):
    step = pl.program_id(0)
    lane = lax.broadcasted_iota(jnp.int32, (C, Z), 1)
    first = lane == 0
    last = lane == Z - 1

    def copies(p):
        if p < 2:
            left, mid, right = clo_ref.at[0, p], xlo_ref.at[p], clo_ref.at[1, p]
        elif p < BX + 2:
            left, mid, right = ylo_ref.at[p - 2], main_ref.at[p - 2], yhi_ref.at[p - 2]
        else:
            q = p - BX - 2
            left, mid, right = chi_ref.at[0, q], xhi_ref.at[q], chi_ref.at[1, q]
        to = raw.at[p]
        return [
            pltpu.make_async_copy(left, to.at[:, 0 : 2 * Z], sems.at[p, 0]),
            pltpu.make_async_copy(mid, to.at[:, 2 * Z : 2 * Z + ROW], sems.at[p, 1]),
            pltpu.make_async_copy(right, to.at[:, 2 * Z + ROW : WIDE], sems.at[p, 2]),
        ]

    def stage(p, xs, y):
        cols = slice(y * Z, (y + 1) * Z)
        v = raw[p, :, cols]
        f = v.astype(jnp.float32)
        xs[0:C, cols] = jnp.where(first, 0.0, pltpu.roll(f, 1, 1)).astype(jnp.bfloat16)
        xs[C : 2 * C, cols] = v
        xs[2 * C : 3 * C, cols] = jnp.where(last, 0.0, pltpu.roll(f, Z - 1, 1)).astype(jnp.bfloat16)

    @pl.when(step == 0)
    def _():
        for p in range(BX + 4):
            for copy in copies(p):
                copy.start()
        for copy in copies(0):
            copy.wait()
        for y in range(BY + 4):
            stage(0, xs_a, y)

    for p in range(1, BX + 4):

        @pl.when(step == (0 if p < 3 else (p - 1) // 2))
        def _():
            for copy in copies(p):
                copy.wait()

    bias = jnp.broadcast_to(bias_ref[...], (C, 2 * Z))
    weights = w_ref[...]

    def half(plane, xs, xs_next, flat, to):
        following = jnp.minimum(plane + 1, BX + 3)
        keep = jnp.where(plane == 2, flags_ref[0], jnp.where(plane == BX + 3, flags_ref[1], 1.0))
        x_out = jnp.clip(plane - 4, 0, BX - 1)
        x_new = jnp.clip(plane - 3, 0, BX - 1)
        before = None
        for t in range((BY + 2) // 2):
            for y in range(2 * t, 2 * t + 2 if t < BY // 2 else BY + 4):
                stage(following, xs_next, y)
            cols = slice(t * 2 * Z, (t + 1) * 2 * Z)
            window = jnp.concatenate(
                [xs[:, (t * 2 + dy) * Z : (t * 2 + dy + 2) * Z] for dy in range(3)], axis=0
            )
            p = jnp.dot(weights, window, preferred_element_type=jnp.float32)
            g = jnp.maximum(acc_b[:, cols] + p[2 * C : 3 * C] + bias, 0.0) * keep
            acc_b[:, cols] = acc_a[:, cols] + p[C : 2 * C]
            acc_a[:, cols] = p[0:C]
            rows = [g[:, :Z], g[:, Z:]]
            if t == 0:
                rows[0] = rows[0] * flags_ref[2]
            if t == BY // 2:
                rows[1] = rows[1] * flags_ref[3]
            if t > 0:
                window4 = before + rows
                for k in range(2):
                    y = 2 * t - 2 + k
                    here = slice(y * Z, (y + 1) * Z)
                    low, mid, high = window4[k], window4[k + 1], window4[k + 2]
                    beside = prev[:, here] + low + high
                    beside = beside + jnp.where(first, 0.0, pltpu.roll(mid, 1, 1))
                    beside = beside + jnp.where(last, 0.0, pltpu.roll(mid, Z - 1, 1))
                    flat[pl.ds(y, C, stride=PITCH), :] = (
                        pend[:, here] + coef_ref[x_out, y : y + 1, :] * mid
                    )
                    pend[:, here] = mid + coef_ref[x_new, y : y + 1, :] * (beside - 6.0 * mid)
                    prev[:, here] = mid
            before = rows
        out_ref[:, to] = flat[...].reshape(C, PITCH, Z)[:, :BY].astype(jnp.bfloat16)

    half(2 * step, xs_a, xs_b, flat_a, 0)
    half(2 * step + 1, xs_b, xs_a, flat_b, 1)


def conv_smooth(flags, weights, bias, coef, main, xlo, xhi, ylo, yhi, clo, chi):
    hbm = pl.BlockSpec(memory_space=pl.ANY)
    return pl.pallas_call(
        conv_kernel,
        grid=((BX + 4) // 2,),
        in_specs=[
            pl.BlockSpec(memory_space=pltpu.SMEM),
            pl.BlockSpec((3 * C, 9 * C), lambda i: (0, 0)),
            pl.BlockSpec((C, 1), lambda i: (0, 0)),
            pl.BlockSpec((BX, BY, Z), lambda i: (0, 0, 0)),
        ]
        + [hbm] * 7,
        out_specs=pl.BlockSpec((C, 2, BY, Z), lambda i: (0, jnp.maximum(i - 2, 0), 0, 0)),
        scratch_shapes=[
            pltpu.VMEM((BX + 4, C, WIDE), jnp.bfloat16),
            pltpu.VMEM((3 * C, WIDE), jnp.bfloat16),
            pltpu.VMEM((3 * C, WIDE), jnp.bfloat16),
            pltpu.VMEM((C, GATED), jnp.float32),
            pltpu.VMEM((C, GATED), jnp.float32),
            pltpu.VMEM((C, ROW), jnp.float32),
            pltpu.VMEM((C, ROW), jnp.float32),
            pltpu.VMEM((C * PITCH, Z), jnp.float32),
            pltpu.VMEM((C * PITCH, Z), jnp.float32),
            pltpu.SemaphoreType.DMA((BX + 4, 3)),
        ],
        out_shape=jax.ShapeDtypeStruct((C, BX, BY, Z), jnp.bfloat16),
        compiler_params=pltpu.CompilerParams(vmem_limit_bytes=56 << 20),
        name="conv_smooth",
    )(flags, weights, bias, coef, main, xlo, xhi, ylo, yhi, clo, chi)


def shift(array, axis, by):
    size = lax.axis_size(axis)
    pairs = [(i, i + by) for i in range(size) if 0 <= i + by < size]
    return lax.ppermute(array, axis, pairs)


def on_device(
    tile_pixel, tile_voxel, tile_count, features, interp, conv_weight, conv_bias, smooth_coef
):
    feats = features[0, 0]
    tiles = interp[0, 0]
    pixel_ids = tile_pixel[0, 0]
    voxel_ids = tile_voxel[0, 0]
    count = tile_count[0, 0]
    slots_total = tiles.shape[0]
    n_bricks = lax.axis_size("bricks")
    n_views = lax.axis_size("views")
    brick = lax.axis_index("bricks")
    view = lax.axis_index("views")
    me = view * n_bricks + brick
    slot_ids = jnp.arange(slots_total, dtype=jnp.int32)
    live = jnp.remainder(slot_ids - jnp.remainder(me * 37, slots_total), slots_total) < count
    mine = jnp.where(live, voxel_ids, BLK).astype(jnp.float32)
    table = lax.psum(
        jnp.where(slot_ids[:, None] == me, mine[None, :], 0.0), ("views", "bricks")
    )
    tgt = lax.dynamic_slice_in_dim(table, me, 1, axis=1)[:, 0].astype(jnp.int32)
    selector = (pixel_ids[:, None] == jnp.arange(feats.shape[0], dtype=jnp.int32)[None, :]).astype(
        jnp.bfloat16
    )
    chosen = jnp.einsum(
        "dk,kq->dq", selector, feats.reshape(feats.shape[0], C * PIX),
        preferred_element_type=jnp.float32,
    )
    chosen = chosen.astype(jnp.bfloat16).reshape(slots_total, C, PIX)
    partial_value = jnp.einsum(
        "dcp,dpv->dcv", chosen, tiles, preferred_element_type=jnp.float32
    ).astype(jnp.bfloat16)
    got = lax.all_to_all(partial_value, ("views", "bricks"), split_axis=0, concat_axis=0, tiled=True)
    main, lo, hi, ylo, yhi = lift(tgt, got)
    from_low = shift(yhi, "views", 1)
    from_high = shift(ylo, "views", -1)
    xlo = shift(hi, "bricks", 1)
    xhi = shift(lo, "bricks", -1)
    clo = shift(jnp.stack([from_low[BX - 2 :], from_high[BX - 2 :]]), "bricks", 1)
    chi = shift(jnp.stack([from_low[:2], from_high[:2]]), "bricks", -1)
    flags = jnp.stack(
        [brick > 0, brick < n_bricks - 1, view > 0, view < n_views - 1]
    ).astype(jnp.float32)
    weights = jnp.transpose(conv_weight, (0, 3, 1, 2, 4)).reshape(3 * C, 9 * C)
    return conv_smooth(
        flags, weights, conv_bias[:, None], smooth_coef, main, xlo, xhi, from_low, from_high, clo, chi
    )


def solution(mesh):
    in_specs = (
        P("views", "bricks", None),
        P("views", "bricks", None),
        P("views", "bricks"),
        P("views", "bricks", None, None, None),
        P("views", "bricks", None, None, None),
        P(),
        P(),
        P("bricks", "views", None),
    )
    out_specs = P(None, "bricks", "views", None)
    return jax.shard_map(
        on_device, mesh=mesh, in_specs=in_specs, out_specs=out_specs, check_vma=False
    )
```

```python
import functools

import jax
import jax.numpy as jnp
from jax import lax
from jax.experimental import pallas as pl
from jax.experimental.pallas import tpu as pltpu
from jax.sharding import PartitionSpec as P

C = 64
PIX = 128
Z = 128
BX = 8
BY = 32
BLK = 64
VOXB = 512
ROW = BY * Z
WIDE = (BY + 4) * Z
GATED = (BY + 2) * Z
SEND = 16
PACK = 4 * C + 8
PITCH = 40


def partial_kernel(pixel_ref, tgt_ref, feats_ref, tiles_ref, out_ref, tiles, out, sems, done):
    chunks = tiles.shape[0] // SEND

    def load(k):
        rows = pl.ds(pl.multiple_of(k * SEND, SEND), SEND)
        return pltpu.make_async_copy(tiles_ref.at[rows], tiles.at[rows], sems.at[k])

    def store(k):
        rows = pl.ds(pl.multiple_of(k * SEND, SEND), SEND)
        return pltpu.make_async_copy(out.at[rows], out_ref.at[rows], done.at[k])

    for k in range(chunks):
        load(k).start()

    def chunk(k, carry):
        load(k).wait()
        for i in range(SEND):
            slot = k * SEND + i
            p = jnp.dot(
                feats_ref[pixel_ref[slot]], tiles[slot], preferred_element_type=jnp.float32
            )
            for q in range(4):
                out[slot, q * C : (q + 1) * C, :] = p[:, q * Z : (q + 1) * Z].astype(jnp.bfloat16)
            block = jnp.full((PACK - 4 * C, Z), tgt_ref[slot].astype(jnp.float32), jnp.float32)
            out[slot, 4 * C : PACK, :] = block.astype(jnp.bfloat16)
        store(k).start()
        return carry

    lax.fori_loop(0, chunks, chunk, 0)
    for k in range(chunks):
        store(k).wait()


def partials(pixel_ids, targets, feats, tiles):
    n = tiles.shape[0]
    smem = pl.BlockSpec(memory_space=pltpu.SMEM)
    hbm = pl.BlockSpec(memory_space=pl.ANY)
    return pl.pallas_call(
        partial_kernel,
        in_specs=[smem, smem, pl.BlockSpec(memory_space=pltpu.VMEM), hbm],
        out_specs=hbm,
        scratch_shapes=[
            pltpu.VMEM((n, PIX, VOXB), jnp.bfloat16),
            pltpu.VMEM((n, PACK, Z), jnp.bfloat16),
            pltpu.SemaphoreType.DMA((n // SEND,)),
            pltpu.SemaphoreType.DMA((n // SEND,)),
        ],
        out_shape=jax.ShapeDtypeStruct((n, PACK, Z), jnp.bfloat16),
        compiler_params=pltpu.CompilerParams(vmem_limit_bytes=48 << 20),
        name="partials",
    )(pixel_ids, targets, feats, tiles)


def lift_kernel(tgt_ref, part_ref, main_ref, lo_ref, hi_ref, ylo_ref, yhi_ref, acc):
    acc[...] = jnp.zeros_like(acc)

    def add(i, carry):
        block = tgt_ref[i]
        acc[block] = acc[block] + part_ref[i, : 4 * C].astype(jnp.float32)
        return carry

    lax.fori_loop(0, part_ref.shape[0], add, 0)

    def plane(x, carry):
        for y in range(BY):
            v = acc[x * (BY // 4) + y // 4, (y % 4) * C : (y % 4 + 1) * C, :]
            v = jnp.maximum(v, 0.0).astype(jnp.bfloat16)
            main_ref[x, :, y * Z : (y + 1) * Z] = v
            if y < 2:
                ylo_ref[x, :, y * Z : (y + 1) * Z] = v
            if y >= BY - 2:
                yhi_ref[x, :, (y - BY + 2) * Z : (y - BY + 3) * Z] = v
        return carry

    lax.fori_loop(0, BX, plane, 0)
    lo_ref[...] = main_ref[0:2]
    hi_ref[...] = main_ref[BX - 2 : BX]


def lift(tgt, part):
    n = part.shape[0]
    vmem = pl.BlockSpec(memory_space=pltpu.VMEM)
    return pl.pallas_call(
        lift_kernel,
        in_specs=[pl.BlockSpec(memory_space=pltpu.SMEM), vmem],
        out_specs=[vmem] * 5,
        scratch_shapes=[
            pltpu.VMEM((BLK + 1, 4 * C, Z), jnp.float32),
        ],
        out_shape=[
            jax.ShapeDtypeStruct((BX, C, ROW), jnp.bfloat16),
            jax.ShapeDtypeStruct((2, C, ROW), jnp.bfloat16),
            jax.ShapeDtypeStruct((2, C, ROW), jnp.bfloat16),
            jax.ShapeDtypeStruct((BX, C, 2 * Z), jnp.bfloat16),
            jax.ShapeDtypeStruct((BX, C, 2 * Z), jnp.bfloat16),
        ],
        compiler_params=pltpu.CompilerParams(vmem_limit_bytes=48 << 20),
        name="lift",
    )(tgt, part)


def conv_kernel(
    flags_ref,
    w_ref,
    bias_ref,
    coef_ref,
    main_ref,
    xlo_ref,
    xhi_ref,
    ylo_ref,
    yhi_ref,
    clo_ref,
    chi_ref,
    out_ref,
    raw,
    xs_a,
    xs_b,
    acc_a,
    acc_b,
    prev,
    pend,
    flat_a,
    flat_b,
    sems,
):
    step = pl.program_id(0)
    lane = lax.broadcasted_iota(jnp.int32, (C, Z), 1)
    first = lane == 0
    last = lane == Z - 1

    def copies(p):
        if p < 2:
            left, mid, right = clo_ref.at[0, p], xlo_ref.at[p], clo_ref.at[1, p]
        elif p < BX + 2:
            left, mid, right = ylo_ref.at[p - 2], main_ref.at[p - 2], yhi_ref.at[p - 2]
        else:
            q = p - BX - 2
            left, mid, right = chi_ref.at[0, q], xhi_ref.at[q], chi_ref.at[1, q]
        to = raw.at[p]
        return [
            pltpu.make_async_copy(left, to.at[:, 0 : 2 * Z], sems.at[p, 0]),
            pltpu.make_async_copy(mid, to.at[:, 2 * Z : 2 * Z + ROW], sems.at[p, 1]),
            pltpu.make_async_copy(right, to.at[:, 2 * Z + ROW : WIDE], sems.at[p, 2]),
        ]

    def stage(p, xs, y):
        cols = slice(y * Z, (y + 1) * Z)
        v = raw[p, :, cols]
        f = v.astype(jnp.float32)
        xs[0:C, cols] = jnp.where(first, 0.0, pltpu.roll(f, 1, 1)).astype(jnp.bfloat16)
        xs[C : 2 * C, cols] = v
        xs[2 * C : 3 * C, cols] = jnp.where(last, 0.0, pltpu.roll(f, Z - 1, 1)).astype(jnp.bfloat16)

    @pl.when(step == 0)
    def _():
        for p in range(BX + 4):
            for copy in copies(p):
                copy.start()
        for copy in copies(0):
            copy.wait()
        for y in range(BY + 4):
            stage(0, xs_a, y)

    for p in range(1, BX + 4):

        @pl.when(step == (0 if p < 3 else (p - 1) // 2))
        def _():
            for copy in copies(p):
                copy.wait()

    bias = jnp.broadcast_to(bias_ref[...], (C, 2 * Z))
    weights = w_ref[...]

    def half(plane, xs, xs_next, flat, to):
        following = jnp.minimum(plane + 1, BX + 3)
        keep = jnp.where(plane == 2, flags_ref[0], jnp.where(plane == BX + 3, flags_ref[1], 1.0))
        x_out = jnp.clip(plane - 4, 0, BX - 1)
        x_new = jnp.clip(plane - 3, 0, BX - 1)
        before = None
        for t in range((BY + 2) // 2):
            for y in range(2 * t, 2 * t + 2 if t < BY // 2 else BY + 4):
                stage(following, xs_next, y)
            cols = slice(t * 2 * Z, (t + 1) * 2 * Z)
            window = jnp.concatenate(
                [xs[:, (t * 2 + dy) * Z : (t * 2 + dy + 2) * Z] for dy in range(3)], axis=0
            )
            p = jnp.dot(weights, window, preferred_element_type=jnp.float32)
            g = jnp.maximum(acc_b[:, cols] + p[2 * C : 3 * C] + bias, 0.0) * keep
            acc_b[:, cols] = acc_a[:, cols] + p[C : 2 * C]
            acc_a[:, cols] = p[0:C]
            rows = [g[:, :Z], g[:, Z:]]
            if t == 0:
                rows[0] = rows[0] * flags_ref[2]
            if t == BY // 2:
                rows[1] = rows[1] * flags_ref[3]
            if t > 0:
                window4 = before + rows
                for k in range(2):
                    y = 2 * t - 2 + k
                    here = slice(y * Z, (y + 1) * Z)
                    low, mid, high = window4[k], window4[k + 1], window4[k + 2]
                    beside = prev[:, here] + low + high
                    beside = beside + jnp.where(first, 0.0, pltpu.roll(mid, 1, 1))
                    beside = beside + jnp.where(last, 0.0, pltpu.roll(mid, Z - 1, 1))
                    flat[pl.ds(y, C, stride=PITCH), :] = (
                        pend[:, here] + coef_ref[x_out, y : y + 1, :] * mid
                    )
                    pend[:, here] = mid + coef_ref[x_new, y : y + 1, :] * (beside - 6.0 * mid)
                    prev[:, here] = mid
            before = rows
        out_ref[:, to] = flat[...].reshape(C, PITCH, Z)[:, :BY].astype(jnp.bfloat16)

    half(2 * step, xs_a, xs_b, flat_a, 0)
    half(2 * step + 1, xs_b, xs_a, flat_b, 1)


def conv_smooth(flags, weights, bias, coef, main, xlo, xhi, ylo, yhi, clo, chi):
    hbm = pl.BlockSpec(memory_space=pl.ANY)
    return pl.pallas_call(
        conv_kernel,
        grid=((BX + 4) // 2,),
        in_specs=[
            pl.BlockSpec(memory_space=pltpu.SMEM),
            pl.BlockSpec((3 * C, 9 * C), lambda i: (0, 0)),
            pl.BlockSpec((C, 1), lambda i: (0, 0)),
            pl.BlockSpec((BX, BY, Z), lambda i: (0, 0, 0)),
        ]
        + [hbm] * 7,
        out_specs=pl.BlockSpec((C, 2, BY, Z), lambda i: (0, jnp.maximum(i - 2, 0), 0, 0)),
        scratch_shapes=[
            pltpu.VMEM((BX + 4, C, WIDE), jnp.bfloat16),
            pltpu.VMEM((3 * C, WIDE), jnp.bfloat16),
            pltpu.VMEM((3 * C, WIDE), jnp.bfloat16),
            pltpu.VMEM((C, GATED), jnp.float32),
            pltpu.VMEM((C, GATED), jnp.float32),
            pltpu.VMEM((C, ROW), jnp.float32),
            pltpu.VMEM((C, ROW), jnp.float32),
            pltpu.VMEM((C * PITCH, Z), jnp.float32),
            pltpu.VMEM((C * PITCH, Z), jnp.float32),
            pltpu.SemaphoreType.DMA((BX + 4, 3)),
        ],
        out_shape=jax.ShapeDtypeStruct((C, BX, BY, Z), jnp.bfloat16),
        compiler_params=pltpu.CompilerParams(vmem_limit_bytes=56 << 20),
        name="conv_smooth",
    )(flags, weights, bias, coef, main, xlo, xhi, ylo, yhi, clo, chi)


def shift(array, axis, by):
    size = lax.axis_size(axis)
    pairs = [(i, i + by) for i in range(size) if 0 <= i + by < size]
    return lax.ppermute(array, axis, pairs)


def on_device(
    tile_pixel, tile_voxel, tile_count, features, interp, conv_weight, conv_bias, smooth_coef
):
    feats = features[0, 0]
    tiles = interp[0, 0]
    pixel_ids = tile_pixel[0, 0]
    voxel_ids = tile_voxel[0, 0]
    count = tile_count[0, 0]
    slots_total = tiles.shape[0]
    n_bricks = lax.axis_size("bricks")
    n_views = lax.axis_size("views")
    brick = lax.axis_index("bricks")
    view = lax.axis_index("views")
    me = view * n_bricks + brick
    slot_ids = jnp.arange(slots_total, dtype=jnp.int32)
    live = jnp.remainder(slot_ids - jnp.remainder(me * 37, slots_total), slots_total) < count
    targets = jnp.where(live, voxel_ids, BLK)
    packed = partials(pixel_ids, targets, feats, tiles)
    got = lax.all_to_all(packed, ("views", "bricks"), split_axis=0, concat_axis=0, tiled=True)
    tgt = got[:, 4 * C, 0].astype(jnp.int32)
    main, lo, hi, ylo, yhi = lift(tgt, got)
    from_low = shift(yhi, "views", 1)
    from_high = shift(ylo, "views", -1)
    xlo = shift(hi, "bricks", 1)
    xhi = shift(lo, "bricks", -1)
    clo = shift(jnp.stack([from_low[BX - 2 :], from_high[BX - 2 :]]), "bricks", 1)
    chi = shift(jnp.stack([from_low[:2], from_high[:2]]), "bricks", -1)
    flags = jnp.stack(
        [brick > 0, brick < n_bricks - 1, view > 0, view < n_views - 1]
    ).astype(jnp.float32)
    weights = jnp.transpose(conv_weight, (0, 3, 1, 2, 4)).reshape(3 * C, 9 * C)
    return conv_smooth(
        flags, weights, conv_bias[:, None], smooth_coef, main, xlo, xhi, from_low, from_high, clo, chi
    )


def solution(mesh):
    in_specs = (
        P("views", "bricks", None),
        P("views", "bricks", None),
        P("views", "bricks"),
        P("views", "bricks", None, None, None),
        P("views", "bricks", None, None, None),
        P(),
        P(),
        P("bricks", "views", None),
    )
    out_specs = P(None, "bricks", "views", None)
    return jax.shard_map(
        on_device, mesh=mesh, in_specs=in_specs, out_specs=out_specs, check_vma=False
    )
```

```python
import functools

import jax
import jax.numpy as jnp
from jax import lax
from jax.experimental import pallas as pl
from jax.experimental.pallas import tpu as pltpu
from jax.sharding import PartitionSpec as P

C = 64
PIX = 128
Z = 128
BX = 8
BY = 32
BLK = 64
VOXB = 512
ROW = BY * Z
WIDE = (BY + 4) * Z
GATED = (BY + 2) * Z
SEND = 16
PACK = 4 * C + 8
PITCH = 40


def partial_kernel(pixel_ref, tgt_ref, feats_ref, tiles_ref, out_ref, tiles, out, sems, done):
    chunks = tiles.shape[0] // SEND

    def load(k):
        rows = pl.ds(pl.multiple_of(k * SEND, SEND), SEND)
        return pltpu.make_async_copy(tiles_ref.at[rows], tiles.at[rows], sems.at[k])

    def store(k):
        rows = pl.ds(pl.multiple_of(k * SEND, SEND), SEND)
        return pltpu.make_async_copy(out.at[rows], out_ref.at[rows], done.at[k])

    for k in range(chunks):
        load(k).start()

    def chunk(k, carry):
        load(k).wait()
        for i in range(SEND):
            slot = k * SEND + i
            p = jnp.dot(
                feats_ref[pixel_ref[slot]], tiles[slot], preferred_element_type=jnp.float32
            )
            for q in range(4):
                out[slot, q * C : (q + 1) * C, :] = p[:, q * Z : (q + 1) * Z].astype(jnp.bfloat16)
            block = jnp.full((PACK - 4 * C, Z), tgt_ref[slot].astype(jnp.float32), jnp.float32)
            out[slot, 4 * C : PACK, :] = block.astype(jnp.bfloat16)
        store(k).start()
        return carry

    lax.fori_loop(0, chunks, chunk, 0)
    for k in range(chunks):
        store(k).wait()


def partials(pixel_ids, targets, feats, tiles):
    n = tiles.shape[0]
    smem = pl.BlockSpec(memory_space=pltpu.SMEM)
    hbm = pl.BlockSpec(memory_space=pl.ANY)
    return pl.pallas_call(
        partial_kernel,
        in_specs=[smem, smem, pl.BlockSpec(memory_space=pltpu.VMEM), hbm],
        out_specs=hbm,
        scratch_shapes=[
            pltpu.VMEM((n, PIX, VOXB), jnp.bfloat16),
            pltpu.VMEM((n, PACK, Z), jnp.bfloat16),
            pltpu.SemaphoreType.DMA((n // SEND,)),
            pltpu.SemaphoreType.DMA((n // SEND,)),
        ],
        out_shape=jax.ShapeDtypeStruct((n, PACK, Z), jnp.bfloat16),
        compiler_params=pltpu.CompilerParams(vmem_limit_bytes=48 << 20),
        name="partials",
    )(pixel_ids, targets, feats, tiles)


def lift_kernel(tgt_ref, part_ref, main_ref, lo_ref, hi_ref, ylo_ref, yhi_ref, acc):
    acc[...] = jnp.zeros_like(acc)

    def add(i, carry):
        block = tgt_ref[i]
        acc[block] = acc[block] + part_ref[i, : 4 * C].astype(jnp.float32)
        return carry

    lax.fori_loop(0, part_ref.shape[0], add, 0)

    def plane(x, carry):
        for y in range(BY):
            v = acc[x * (BY // 4) + y // 4, (y % 4) * C : (y % 4 + 1) * C, :]
            v = jnp.maximum(v, 0.0).astype(jnp.bfloat16)
            main_ref[x, :, y * Z : (y + 1) * Z] = v
            if y < 2:
                ylo_ref[x, :, y * Z : (y + 1) * Z] = v
            if y >= BY - 2:
                yhi_ref[x, :, (y - BY + 2) * Z : (y - BY + 3) * Z] = v
        return carry

    lax.fori_loop(0, BX, plane, 0)
    lo_ref[...] = main_ref[0:2]
    hi_ref[...] = main_ref[BX - 2 : BX]


def lift(tgt, part):
    n = part.shape[0]
    vmem = pl.BlockSpec(memory_space=pltpu.VMEM)
    return pl.pallas_call(
        lift_kernel,
        in_specs=[pl.BlockSpec(memory_space=pltpu.SMEM), vmem],
        out_specs=[vmem] * 5,
        scratch_shapes=[
            pltpu.VMEM((BLK + 1, 4 * C, Z), jnp.float32),
        ],
        out_shape=[
            jax.ShapeDtypeStruct((BX, C, ROW), jnp.bfloat16),
            jax.ShapeDtypeStruct((2, C, ROW), jnp.bfloat16),
            jax.ShapeDtypeStruct((2, C, ROW), jnp.bfloat16),
            jax.ShapeDtypeStruct((BX, C, 2 * Z), jnp.bfloat16),
            jax.ShapeDtypeStruct((BX, C, 2 * Z), jnp.bfloat16),
        ],
        compiler_params=pltpu.CompilerParams(vmem_limit_bytes=48 << 20),
        name="lift",
    )(tgt, part)


def shifted(v, first, last):
    down = jnp.where(first, 0.0, pltpu.roll(v, 1, 1))
    up = jnp.where(last, 0.0, pltpu.roll(v, Z - 1, 1))
    return down, up


def edges():
    lane = lax.broadcasted_iota(jnp.int32, (C, Z), 1)
    return lane == 0, lane == Z - 1


def stage(raw, p, xs, y, ends):
    cols = slice(y * Z, (y + 1) * Z)
    v = raw[p, :, cols]
    down, up = shifted(v.astype(jnp.float32), *ends)
    xs[0:C, cols] = down.astype(jnp.bfloat16)
    xs[C : 2 * C, cols] = v
    xs[2 * C : 3 * C, cols] = up.astype(jnp.bfloat16)


def stage_rows(t):
    return range(2 * t, 2 * t + 2 if t < BY // 2 else BY + 4)


def window(xs, t):
    return jnp.concatenate(
        [xs[:, (t * 2 + dy) * Z : (t * 2 + dy + 2) * Z] for dy in range(3)], axis=0
    )


def split_rows(g, t, flags_ref):
    rows = [g[:, :Z], g[:, Z:]]
    if t == 0:
        rows[0] = rows[0] * flags_ref[2]
    if t == BY // 2:
        rows[1] = rows[1] * flags_ref[3]
    return rows


def plane_copies(left, mid, right, to, sems):
    return [
        pltpu.make_async_copy(left, to.at[:, 0 : 2 * Z], sems.at[0]),
        pltpu.make_async_copy(mid, to.at[:, 2 * Z : 2 * Z + ROW], sems.at[1]),
        pltpu.make_async_copy(right, to.at[:, 2 * Z + ROW : WIDE], sems.at[2]),
    ]


def inner_kernel(
    flags_ref, w_ref, bias_ref, coef_ref, main_ref, ylo_ref, yhi_ref,
    out_ref, outer_ref, edge_ref, near_ref, pend_ref,
    raw, xs_a, xs_b, acc_a, acc_b, prev, pend, flat_a, flat_b, packed, sems, done,
):
    ends = edges()
    copies = [
        plane_copies(ylo_ref.at[x], main_ref.at[x], yhi_ref.at[x], raw.at[x], sems.at[x])
        for x in range(BX)
    ]
    stores = [
        pltpu.make_async_copy(packed.at[k], out_ref.at[:, k + 2], done.at[k])
        for k in range(BX - 4)
    ]
    for group in copies:
        for copy in group:
            copy.start()
    bias = jnp.broadcast_to(bias_ref[...], (C, 2 * Z))
    weights = w_ref[...]
    buffers, flats = (xs_a, xs_b), (flat_a, flat_b)
    for copy in copies[0]:
        copy.wait()
    for y in range(BY + 4):
        stage(raw, 0, xs_a, y, ends)
    for x in range(BX):
        xs, xs_next, flat = buffers[x % 2], buffers[(x + 1) % 2], flats[x % 2]
        if x + 1 < BX:
            for copy in copies[x + 1]:
                copy.wait()
        new = x - 1
        before = None
        for t in range((BY + 2) // 2):
            if x + 1 < BX:
                for y in stage_rows(t):
                    stage(raw, x + 1, xs_next, y, ends)
            cols = slice(t * 2 * Z, (t + 1) * 2 * Z)
            p = jnp.dot(weights, window(xs, t), preferred_element_type=jnp.float32)
            if x == 0:
                outer_ref[0, :, cols] = p[2 * C :]
                acc_b[:, cols] = p[C : 2 * C]
                acc_a[:, cols] = p[:C]
                continue
            total = acc_b[:, cols] + p[2 * C :]
            if x == BX - 1:
                edge_ref[1, :, cols] = acc_a[:, cols] + p[C : 2 * C]
                outer_ref[1, :, cols] = p[:C]
            else:
                acc_b[:, cols] = acc_a[:, cols] + p[C : 2 * C]
                acc_a[:, cols] = p[:C]
            if x == 1:
                edge_ref[0, :, cols] = total
                continue
            rows = split_rows(jnp.maximum(total + bias, 0.0), t, flags_ref)
            if t > 0:
                four = before + rows
                for k in range(2):
                    y = 2 * t - 2 + k
                    here = slice(y * Z, (y + 1) * Z)
                    low, mid, high = four[k], four[k + 1], four[k + 2]
                    down, up = shifted(mid, *ends)
                    beside = low + high + down + up
                    if new > 1:
                        beside = beside + prev[:, here]
                        full = pend[:, here] + coef_ref[new - 1, y : y + 1, :] * mid
                        if new == 2:
                            pend_ref[0, :, here] = full
                        else:
                            flat[pl.ds(y, C, stride=PITCH), :] = full
                    later = mid + coef_ref[new, y : y + 1, :] * (beside - 6.0 * mid)
                    if new == 1:
                        near_ref[0, :, here] = mid
                    if new == BX - 2:
                        near_ref[1, :, here] = mid
                        pend_ref[1, :, here] = later
                    else:
                        prev[:, here] = mid
                        pend[:, here] = later
            before = rows
        if new > 2:
            packed[new - 3] = flat[...].reshape(C, PITCH, Z)[:, :BY].astype(jnp.bfloat16)
            stores[new - 3].start()
    for copy in stores:
        copy.wait()


def outer_kernel(
    flags_ref, w_ref, bias_ref, coef_ref, outer_ref, edge_ref, near_ref, pend_ref,
    xlo_ref, xhi_ref, clo_ref, chi_ref, part_ref,
    out_ref,
    raw, xs_0, xs_1, xs_2, xs_3, flat_a, flat_b, packed, sems, done,
):
    ends = edges()
    copies = []
    for p, (face, corner, q) in enumerate(
        [(xlo_ref, clo_ref, 0), (xlo_ref, clo_ref, 1), (xhi_ref, chi_ref, 1), (xhi_ref, chi_ref, 0)]
    ):
        copies.append(
            plane_copies(corner.at[0, q], face.at[q], corner.at[1, q], raw.at[p], sems.at[p])
        )
        for copy in copies[p]:
            copy.start()
    targets = [(0, 1), (BX - 1, BX - 2)]
    stores = [
        [
            pltpu.make_async_copy(packed.at[2 * s + k], out_ref.at[:, targets[s][k]], done.at[s, k])
            for k in range(2)
        ]
        for s in range(2)
    ]
    bias = jnp.broadcast_to(bias_ref[...], (C, 2 * Z))
    planes = (xs_0, xs_1, xs_2, xs_3)
    for p in range(2):
        for copy in copies[p]:
            copy.wait()
        for y in range(BY + 4):
            stage(raw, p, planes[p], y, ends)
    for s in range(2):
        far, nearer = planes[2 * s], planes[2 * s + 1]
        e, i = targets[s]
        if s == 0:
            for p in (2, 3):
                for copy in copies[p]:
                    copy.wait()
        before = None
        for t in range((BY + 2) // 2):
            if s == 0:
                for p in (2, 3):
                    for y in stage_rows(t):
                        stage(raw, p, planes[p], y, ends)
            cols = slice(t * 2 * Z, (t + 1) * 2 * Z)
            a = jnp.dot(w_ref[s, :C], window(far, t), preferred_element_type=jnp.float32)
            b = jnp.dot(w_ref[s, C:], window(nearer, t), preferred_element_type=jnp.float32)
            past = jnp.maximum(outer_ref[s, :, cols] + a + b[:C] + bias, 0.0) * flags_ref[s]
            rows = split_rows(
                jnp.maximum(edge_ref[s, :, cols] + b[C:] + bias, 0.0), t, flags_ref
            )
            past = [past[:, :Z], past[:, Z:]]
            if t > 0:
                four = before[0] + rows
                two = [before[1][1], past[0]]
                for k in range(2):
                    y = 2 * t - 2 + k
                    here = slice(y * Z, (y + 1) * Z)
                    low, mid, high = four[k], four[k + 1], four[k + 2]
                    down, up = shifted(mid, *ends)
                    beside = low + high + down + up + two[k] + near_ref[s, :, here]
                    flat_a[pl.ds(y, C, stride=PITCH), :] = mid + coef_ref[e, y : y + 1, :] * (
                        beside - 6.0 * mid
                    )
                    flat_b[pl.ds(y, C, stride=PITCH), :] = (
                        pend_ref[s, :, here] + coef_ref[i, y : y + 1, :] * mid
                    )
            before = (rows, past)
        for k, flat in enumerate((flat_a, flat_b)):
            packed[2 * s + k] = flat[...].reshape(C, PITCH, Z)[:, :BY].astype(jnp.bfloat16)
            stores[s][k].start()
    for group in stores:
        for copy in group:
            copy.wait()


def conv_inner(flags, weights, bias, coef, main, ylo, yhi):
    hbm = pl.BlockSpec(memory_space=pl.ANY)
    vmem = pl.BlockSpec(memory_space=pltpu.VMEM)
    state = lambda width: jax.ShapeDtypeStruct((2, C, width), jnp.float32)
    return pl.pallas_call(
        inner_kernel,
        in_specs=[pl.BlockSpec(memory_space=pltpu.SMEM), vmem, vmem, vmem, hbm, hbm, hbm],
        out_specs=[hbm] + [vmem] * 4,
        scratch_shapes=[
            pltpu.VMEM((BX, C, WIDE), jnp.bfloat16),
            pltpu.VMEM((3 * C, WIDE), jnp.bfloat16),
            pltpu.VMEM((3 * C, WIDE), jnp.bfloat16),
            pltpu.VMEM((C, GATED), jnp.float32),
            pltpu.VMEM((C, GATED), jnp.float32),
            pltpu.VMEM((C, ROW), jnp.float32),
            pltpu.VMEM((C, ROW), jnp.float32),
            pltpu.VMEM((C * PITCH, Z), jnp.float32),
            pltpu.VMEM((C * PITCH, Z), jnp.float32),
            pltpu.VMEM((BX - 4, C, BY, Z), jnp.bfloat16),
            pltpu.SemaphoreType.DMA((BX, 3)),
            pltpu.SemaphoreType.DMA((BX - 4,)),
        ],
        out_shape=[
            jax.ShapeDtypeStruct((C, BX, BY, Z), jnp.bfloat16),
            state(GATED),
            state(GATED),
            state(ROW),
            state(ROW),
        ],
        compiler_params=pltpu.CompilerParams(vmem_limit_bytes=48 << 20),
        name="conv_inner",
    )(flags, weights, bias, coef, main, ylo, yhi)


def conv_outer(flags, weights, bias, coef, state, xlo, xhi, clo, chi, volume):
    hbm = pl.BlockSpec(memory_space=pl.ANY)
    vmem = pl.BlockSpec(memory_space=pltpu.VMEM)
    return pl.pallas_call(
        outer_kernel,
        in_specs=[pl.BlockSpec(memory_space=pltpu.SMEM)] + [vmem] * 7 + [hbm] * 5,
        out_specs=hbm,
        scratch_shapes=[pltpu.VMEM((4, C, WIDE), jnp.bfloat16)]
        + [pltpu.VMEM((3 * C, WIDE), jnp.bfloat16)] * 4
        + [pltpu.VMEM((C * PITCH, Z), jnp.float32)] * 2
        + [
            pltpu.VMEM((4, C, BY, Z), jnp.bfloat16),
            pltpu.SemaphoreType.DMA((4, 3)),
            pltpu.SemaphoreType.DMA((2, 2)),
        ],
        out_shape=jax.ShapeDtypeStruct((C, BX, BY, Z), jnp.bfloat16),
        input_output_aliases={12: 0},
        compiler_params=pltpu.CompilerParams(vmem_limit_bytes=48 << 20),
        name="conv_outer",
    )(flags, weights, bias, coef, *state, xlo, xhi, clo, chi, volume)


def shift(array, axis, by):
    size = lax.axis_size(axis)
    pairs = [(i, i + by) for i in range(size) if 0 <= i + by < size]
    return lax.ppermute(array, axis, pairs)


def on_device(
    tile_pixel, tile_voxel, tile_count, features, interp, conv_weight, conv_bias, smooth_coef
):
    feats = features[0, 0]
    tiles = interp[0, 0]
    pixel_ids = tile_pixel[0, 0]
    voxel_ids = tile_voxel[0, 0]
    count = tile_count[0, 0]
    slots_total = tiles.shape[0]
    n_bricks = lax.axis_size("bricks")
    n_views = lax.axis_size("views")
    brick = lax.axis_index("bricks")
    view = lax.axis_index("views")
    me = view * n_bricks + brick
    slot_ids = jnp.arange(slots_total, dtype=jnp.int32)
    live = jnp.remainder(slot_ids - jnp.remainder(me * 37, slots_total), slots_total) < count
    targets = jnp.where(live, voxel_ids, BLK)
    packed = partials(pixel_ids, targets, feats, tiles)
    got = lax.all_to_all(packed, ("views", "bricks"), split_axis=0, concat_axis=0, tiled=True)
    tgt = got[:, 4 * C, 0].astype(jnp.int32)
    main, lo, hi, ylo, yhi = lift(tgt, got)
    from_low = shift(yhi, "views", 1)
    from_high = shift(ylo, "views", -1)
    xlo = shift(hi, "bricks", 1)
    xhi = shift(lo, "bricks", -1)
    clo = shift(jnp.stack([from_low[BX - 2 :], from_high[BX - 2 :]]), "bricks", 1)
    chi = shift(jnp.stack([from_low[:2], from_high[:2]]), "bricks", -1)
    flags = jnp.stack(
        [brick > 0, brick < n_bricks - 1, view > 0, view < n_views - 1]
    ).astype(jnp.float32)
    weights = jnp.transpose(conv_weight, (0, 3, 1, 2, 4)).reshape(3 * C, 9 * C)
    sides = jnp.stack(
        [
            jnp.concatenate([weights[:C], weights[C : 2 * C], weights[:C]]),
            jnp.concatenate([weights[2 * C :], weights[C : 2 * C], weights[2 * C :]]),
        ]
    )
    bias = conv_bias[:, None]
    volume, *state = conv_inner(flags, weights, bias, smooth_coef, main, from_low, from_high)
    return conv_outer(flags, sides, bias, smooth_coef, state, xlo, xhi, clo, chi, volume)


def solution(mesh):
    in_specs = (
        P("views", "bricks", None),
        P("views", "bricks", None),
        P("views", "bricks"),
        P("views", "bricks", None, None, None),
        P("views", "bricks", None, None, None),
        P(),
        P(),
        P("bricks", "views", None),
    )
    out_specs = P(None, "bricks", "views", None)
    return jax.shard_map(
        on_device, mesh=mesh, in_specs=in_specs, out_specs=out_specs, check_vma=False
    )
```

```python
import functools

import jax
import jax.numpy as jnp
from jax import lax
from jax.experimental import pallas as pl
from jax.experimental.pallas import tpu as pltpu
from jax.sharding import PartitionSpec as P

C = 64
PIX = 128
Z = 128
BX = 8
BY = 32
BLK = 64
VOXB = 512
ROW = BY * Z
WIDE = (BY + 4) * Z
GATED = (BY + 2) * Z
SEND = 16
PACK = 4 * C + 8
PITCH = 40


def partial_kernel(
    pixel_ref, voxel_ref, count_ref, feats_ref, cw_ref, cb_ref, tiles_ref,
    out_ref, w_ref, bias_ref,
    tiles, out, sems, done,
):
    chunks = tiles.shape[0] // SEND

    def load(k):
        rows = pl.ds(pl.multiple_of(k * SEND, SEND), SEND)
        return pltpu.make_async_copy(tiles_ref.at[rows], tiles.at[rows], sems.at[k])

    def store(k):
        rows = pl.ds(pl.multiple_of(k * SEND, SEND), SEND)
        return pltpu.make_async_copy(out.at[rows], out_ref.at[rows], done.at[k])

    for k in range(chunks):
        load(k).start()

    taps = 9
    for dx in range(3):
        for q in range(0, taps, 2):
            pieces = [cw_ref[dx * taps + r] for r in range(q, min(q + 2, taps))]
            both = pieces[0] if len(pieces) == 1 else jnp.concatenate(pieces, axis=1)
            w_ref[dx * C : (dx + 1) * C, q * C : q * C + both.shape[1]] = both
    eye = lax.broadcasted_iota(jnp.int32, (C, C), 0) == lax.broadcasted_iota(jnp.int32, (C, C), 1)
    column = jnp.where(eye, jnp.broadcast_to(cb_ref[...], (C, C)), 0.0)
    bias_ref[...] = jnp.broadcast_to(jnp.sum(column, axis=1, keepdims=True), (C, 2 * Z))
    me = lax.axis_index("views") * lax.axis_size("bricks") + lax.axis_index("bricks")
    slots = tiles.shape[0]
    offset = lax.rem(me * 37, slots)
    count = count_ref[0]

    def chunk(k, carry):
        load(k).wait()
        for i in range(SEND):
            slot = k * SEND + i
            p = jnp.dot(
                feats_ref[pixel_ref[slot]], tiles[slot], preferred_element_type=jnp.float32
            )
            for q in range(4):
                out[slot, q * C : (q + 1) * C, :] = p[:, q * Z : (q + 1) * Z].astype(jnp.bfloat16)
            place = slot - offset
            place = jnp.where(place < 0, place + slots, place)
            target = jnp.where(place < count, voxel_ref[slot], BLK)
            block = jnp.full((PACK - 4 * C, Z), target.astype(jnp.float32), jnp.float32)
            out[slot, 4 * C : PACK, :] = block.astype(jnp.bfloat16)
        store(k).start()
        return carry

    lax.fori_loop(0, chunks, chunk, 0)
    for k in range(chunks):
        store(k).wait()


def partials(pixel_ids, voxel_ids, count, feats, conv_weight, conv_bias, tiles):
    n = tiles.shape[0]
    smem = pl.BlockSpec(memory_space=pltpu.SMEM)
    vmem = pl.BlockSpec(memory_space=pltpu.VMEM)
    hbm = pl.BlockSpec(memory_space=pl.ANY)
    return pl.pallas_call(
        partial_kernel,
        in_specs=[smem, smem, smem, vmem, vmem, vmem, hbm],
        out_specs=[hbm, vmem, vmem],
        scratch_shapes=[
            pltpu.VMEM((n, PIX, VOXB), jnp.bfloat16),
            pltpu.VMEM((n, PACK, Z), jnp.bfloat16),
            pltpu.SemaphoreType.DMA((n // SEND,)),
            pltpu.SemaphoreType.DMA((n // SEND,)),
        ],
        out_shape=[
            jax.ShapeDtypeStruct((n, PACK, Z), jnp.bfloat16),
            jax.ShapeDtypeStruct((3 * C, 9 * C), jnp.bfloat16),
            jax.ShapeDtypeStruct((C, 2 * Z), jnp.float32),
        ],
        compiler_params=pltpu.CompilerParams(vmem_limit_bytes=48 << 20),
        name="partials",
    )(pixel_ids, voxel_ids, count, feats, conv_weight, conv_bias, tiles)


def lift_kernel(
    part_ref, main_ref, lo_ref, hi_ref, ylo_ref, yhi_ref, acc, rows, ids, tgt_ref, sem, done
):
    n = part_ref.shape[0]
    lane = lax.broadcasted_iota(jnp.int32, (8, Z), 1)
    table = jnp.zeros((8, Z), jnp.float32)
    for i in range(n):
        table = jnp.where(lane == i, part_ref[i, 4 * C : PACK].astype(jnp.float32), table)
    ids[...] = table.astype(jnp.int32)
    move = pltpu.make_async_copy(ids, tgt_ref, sem)
    move.start()
    acc[...] = jnp.zeros_like(acc)
    move.wait()

    def add(i, carry):
        block = tgt_ref[0, i]

        @pl.when(block < BLK)
        def _():
            acc[block] = acc[block] + part_ref[i, : 4 * C].astype(jnp.float32)

        return carry

    lax.fori_loop(0, n, add, 0)

    stores = [pltpu.make_async_copy(rows.at[x], main_ref.at[x], done.at[x]) for x in range(BX)]
    for x in range(BX):
        for y in range(BY):
            v = acc[x * (BY // 4) + y // 4, (y % 4) * C : (y % 4 + 1) * C, :]
            v = jnp.maximum(v, 0.0).astype(jnp.bfloat16)
            cols = slice(y * Z, (y + 1) * Z)
            rows[x, :, cols] = v
            if x < 2:
                lo_ref[x, :, cols] = v
            if x >= BX - 2:
                hi_ref[x - BX + 2, :, cols] = v
            if y < 2:
                ylo_ref[x, :, cols] = v
            if y >= BY - 2:
                yhi_ref[x, :, (y - BY + 2) * Z : (y - BY + 3) * Z] = v
        stores[x].start()
    for copy in stores:
        copy.wait()


def lift(part):
    vmem = pl.BlockSpec(memory_space=pltpu.VMEM)
    return pl.pallas_call(
        lift_kernel,
        in_specs=[vmem],
        out_specs=[pl.BlockSpec(memory_space=pl.ANY)] + [vmem] * 4,
        scratch_shapes=[
            pltpu.VMEM((BLK, 4 * C, Z), jnp.float32),
            pltpu.VMEM((BX, C, ROW), jnp.bfloat16),
            pltpu.VMEM((8, Z), jnp.int32),
            pltpu.SMEM((8, Z), jnp.int32),
            pltpu.SemaphoreType.DMA,
            pltpu.SemaphoreType.DMA((BX,)),
        ],
        out_shape=[
            jax.ShapeDtypeStruct((BX, C, ROW), jnp.bfloat16),
            jax.ShapeDtypeStruct((2, C, ROW), jnp.bfloat16),
            jax.ShapeDtypeStruct((2, C, ROW), jnp.bfloat16),
            jax.ShapeDtypeStruct((BX, C, 2 * Z), jnp.bfloat16),
            jax.ShapeDtypeStruct((BX, C, 2 * Z), jnp.bfloat16),
        ],
        compiler_params=pltpu.CompilerParams(vmem_limit_bytes=48 << 20),
        name="lift",
    )(part)


def inside():
    brick, view = lax.axis_index("bricks"), lax.axis_index("views")
    return [
        jnp.where(test, 1.0, 0.0).astype(jnp.float32)
        for test in (
            brick > 0,
            brick < lax.axis_size("bricks") - 1,
            view > 0,
            view < lax.axis_size("views") - 1,
        )
    ]


def shifted(v, first, last):
    down = jnp.where(first, 0.0, pltpu.roll(v, 1, 1))
    up = jnp.where(last, 0.0, pltpu.roll(v, Z - 1, 1))
    return down, up


def edges():
    lane = lax.broadcasted_iota(jnp.int32, (C, Z), 1)
    return lane == 0, lane == Z - 1


def stage(raw, p, xs, y, ends):
    cols = slice(y * Z, (y + 1) * Z)
    v = raw[p, :, cols]
    down, up = shifted(v.astype(jnp.float32), *ends)
    xs[0:C, cols] = down.astype(jnp.bfloat16)
    xs[C : 2 * C, cols] = v
    xs[2 * C : 3 * C, cols] = up.astype(jnp.bfloat16)


def stage_rows(t):
    return range(2 * t, 2 * t + 2 if t < BY // 2 else BY + 4)


def window(xs, t):
    return jnp.concatenate(
        [xs[:, (t * 2 + dy) * Z : (t * 2 + dy + 2) * Z] for dy in range(3)], axis=0
    )


def split_rows(g, t, flags):
    rows = [g[:, :Z], g[:, Z:]]
    if t == 0:
        rows[0] = rows[0] * flags[2]
    if t == BY // 2:
        rows[1] = rows[1] * flags[3]
    return rows


def plane_copies(left, mid, right, to, sems):
    return [
        pltpu.make_async_copy(left, to.at[:, 0 : 2 * Z], sems.at[0]),
        pltpu.make_async_copy(mid, to.at[:, 2 * Z : 2 * Z + ROW], sems.at[1]),
        pltpu.make_async_copy(right, to.at[:, 2 * Z + ROW : WIDE], sems.at[2]),
    ]


def inner_kernel(
    w_ref, bias_ref, coef_ref, main_ref, ylo_ref, yhi_ref,
    out_ref, outer_ref, edge_ref, near_ref, pend_ref,
    raw, xs_a, xs_b, acc_a, acc_b, prev, pend, flat_a, flat_b, packed, sems, done,
):
    ends, flags = edges(), inside()
    copies = [
        plane_copies(ylo_ref.at[x], main_ref.at[x], yhi_ref.at[x], raw.at[x], sems.at[x])
        for x in range(BX)
    ]
    stores = [
        pltpu.make_async_copy(packed.at[k], out_ref.at[:, k + 2], done.at[k])
        for k in range(BX - 4)
    ]
    for group in copies:
        for copy in group:
            copy.start()
    bias = bias_ref[...]
    weights = w_ref[...]
    buffers, flats = (xs_a, xs_b), (flat_a, flat_b)
    for copy in copies[0]:
        copy.wait()
    for y in range(BY + 4):
        stage(raw, 0, xs_a, y, ends)
    for x in range(BX):
        xs, xs_next, flat = buffers[x % 2], buffers[(x + 1) % 2], flats[x % 2]
        if x + 1 < BX:
            for copy in copies[x + 1]:
                copy.wait()
        new = x - 1
        before = None
        for t in range((BY + 2) // 2):
            if x + 1 < BX:
                for y in stage_rows(t):
                    stage(raw, x + 1, xs_next, y, ends)
            cols = slice(t * 2 * Z, (t + 1) * 2 * Z)
            p = jnp.dot(weights, window(xs, t), preferred_element_type=jnp.float32)
            if x == 0:
                outer_ref[0, :, cols] = p[2 * C :]
                acc_b[:, cols] = p[C : 2 * C]
                acc_a[:, cols] = p[:C]
                continue
            total = acc_b[:, cols] + p[2 * C :]
            if x == BX - 1:
                edge_ref[1, :, cols] = acc_a[:, cols] + p[C : 2 * C]
                outer_ref[1, :, cols] = p[:C]
            else:
                acc_b[:, cols] = acc_a[:, cols] + p[C : 2 * C]
                acc_a[:, cols] = p[:C]
            if x == 1:
                edge_ref[0, :, cols] = total
                continue
            rows = split_rows(jnp.maximum(total + bias, 0.0), t, flags)
            if t > 0:
                four = before + rows
                for k in range(2):
                    y = 2 * t - 2 + k
                    here = slice(y * Z, (y + 1) * Z)
                    low, mid, high = four[k], four[k + 1], four[k + 2]
                    down, up = shifted(mid, *ends)
                    beside = low + high + down + up
                    if new > 1:
                        beside = beside + prev[:, here]
                        full = pend[:, here] + coef_ref[new - 1, y : y + 1, :] * mid
                        if new == 2:
                            pend_ref[0, :, here] = full
                        else:
                            flat[pl.ds(y, C, stride=PITCH), :] = full
                    later = mid + coef_ref[new, y : y + 1, :] * (beside - 6.0 * mid)
                    if new == 1:
                        near_ref[0, :, here] = mid
                    if new == BX - 2:
                        near_ref[1, :, here] = mid
                        pend_ref[1, :, here] = later
                    else:
                        prev[:, here] = mid
                        pend[:, here] = later
            before = rows
        if new > 2:
            packed[new - 3] = flat[...].reshape(C, PITCH, Z)[:, :BY].astype(jnp.bfloat16)
            stores[new - 3].start()
    for copy in stores:
        copy.wait()


def outer_kernel(
    w_ref, bias_ref, coef_ref, outer_ref, edge_ref, near_ref, pend_ref,
    xlo_ref, xhi_ref, clo_ref, chi_ref, part_ref,
    out_ref,
    raw, xs_0, xs_1, xs_2, xs_3, flat_a, flat_b, packed, sems, done,
):
    ends, flags = edges(), inside()
    copies = []
    for p, (face, corner, q) in enumerate(
        [(xlo_ref, clo_ref, 0), (xlo_ref, clo_ref, 1), (xhi_ref, chi_ref, 1), (xhi_ref, chi_ref, 0)]
    ):
        copies.append(
            plane_copies(corner.at[0, q], face.at[q], corner.at[1, q], raw.at[p], sems.at[p])
        )
        for copy in copies[p]:
            copy.start()
    targets = [(0, 1), (BX - 1, BX - 2)]
    stores = [
        [
            pltpu.make_async_copy(packed.at[2 * s + k], out_ref.at[:, targets[s][k]], done.at[s, k])
            for k in range(2)
        ]
        for s in range(2)
    ]
    bias = bias_ref[...]
    planes = (xs_0, xs_1, xs_2, xs_3)
    for p in range(2):
        for copy in copies[p]:
            copy.wait()
        for y in range(BY + 4):
            stage(raw, p, planes[p], y, ends)
    for s in range(2):
        far, nearer = planes[2 * s], planes[2 * s + 1]
        w_side = w_ref[2 * s * C : (2 * s + 1) * C]
        w_both = jnp.concatenate([w_ref[C : 2 * C], w_side], axis=0)
        e, i = targets[s]
        if s == 0:
            for p in (2, 3):
                for copy in copies[p]:
                    copy.wait()
        before = None
        for t in range((BY + 2) // 2):
            if s == 0:
                for p in (2, 3):
                    for y in stage_rows(t):
                        stage(raw, p, planes[p], y, ends)
            cols = slice(t * 2 * Z, (t + 1) * 2 * Z)
            a = jnp.dot(w_side, window(far, t), preferred_element_type=jnp.float32)
            b = jnp.dot(w_both, window(nearer, t), preferred_element_type=jnp.float32)
            past = jnp.maximum(outer_ref[s, :, cols] + a + b[:C] + bias, 0.0) * flags[s]
            rows = split_rows(
                jnp.maximum(edge_ref[s, :, cols] + b[C:] + bias, 0.0), t, flags
            )
            past = [past[:, :Z], past[:, Z:]]
            if t > 0:
                four = before[0] + rows
                two = [before[1][1], past[0]]
                for k in range(2):
                    y = 2 * t - 2 + k
                    here = slice(y * Z, (y + 1) * Z)
                    low, mid, high = four[k], four[k + 1], four[k + 2]
                    down, up = shifted(mid, *ends)
                    beside = low + high + down + up + two[k] + near_ref[s, :, here]
                    flat_a[pl.ds(y, C, stride=PITCH), :] = mid + coef_ref[e, y : y + 1, :] * (
                        beside - 6.0 * mid
                    )
                    flat_b[pl.ds(y, C, stride=PITCH), :] = (
                        pend_ref[s, :, here] + coef_ref[i, y : y + 1, :] * mid
                    )
            before = (rows, past)
        for k, flat in enumerate((flat_a, flat_b)):
            packed[2 * s + k] = flat[...].reshape(C, PITCH, Z)[:, :BY].astype(jnp.bfloat16)
            stores[s][k].start()
    for group in stores:
        for copy in group:
            copy.wait()


def conv_inner(weights, bias, coef, main, ylo, yhi):
    hbm = pl.BlockSpec(memory_space=pl.ANY)
    vmem = pl.BlockSpec(memory_space=pltpu.VMEM)
    state = lambda width: jax.ShapeDtypeStruct((2, C, width), jnp.float32)
    return pl.pallas_call(
        inner_kernel,
        in_specs=[vmem, vmem, vmem, hbm, hbm, hbm],
        out_specs=[hbm] + [vmem] * 4,
        scratch_shapes=[
            pltpu.VMEM((BX, C, WIDE), jnp.bfloat16),
            pltpu.VMEM((3 * C, WIDE), jnp.bfloat16),
            pltpu.VMEM((3 * C, WIDE), jnp.bfloat16),
            pltpu.VMEM((C, GATED), jnp.float32),
            pltpu.VMEM((C, GATED), jnp.float32),
            pltpu.VMEM((C, ROW), jnp.float32),
            pltpu.VMEM((C, ROW), jnp.float32),
            pltpu.VMEM((C * PITCH, Z), jnp.float32),
            pltpu.VMEM((C * PITCH, Z), jnp.float32),
            pltpu.VMEM((BX - 4, C, BY, Z), jnp.bfloat16),
            pltpu.SemaphoreType.DMA((BX, 3)),
            pltpu.SemaphoreType.DMA((BX - 4,)),
        ],
        out_shape=[
            jax.ShapeDtypeStruct((C, BX, BY, Z), jnp.bfloat16),
            state(GATED),
            state(GATED),
            state(ROW),
            state(ROW),
        ],
        compiler_params=pltpu.CompilerParams(vmem_limit_bytes=48 << 20),
        name="conv_inner",
    )(weights, bias, coef, main, ylo, yhi)


def conv_outer(weights, bias, coef, state, xlo, xhi, clo, chi, volume):
    hbm = pl.BlockSpec(memory_space=pl.ANY)
    vmem = pl.BlockSpec(memory_space=pltpu.VMEM)
    return pl.pallas_call(
        outer_kernel,
        in_specs=[vmem] * 7 + [hbm] * 5,
        out_specs=hbm,
        scratch_shapes=[pltpu.VMEM((4, C, WIDE), jnp.bfloat16)]
        + [pltpu.VMEM((3 * C, WIDE), jnp.bfloat16)] * 4
        + [pltpu.VMEM((C * PITCH, Z), jnp.float32)] * 2
        + [
            pltpu.VMEM((4, C, BY, Z), jnp.bfloat16),
            pltpu.SemaphoreType.DMA((4, 3)),
            pltpu.SemaphoreType.DMA((2, 2)),
        ],
        out_shape=jax.ShapeDtypeStruct((C, BX, BY, Z), jnp.bfloat16),
        input_output_aliases={11: 0},
        compiler_params=pltpu.CompilerParams(vmem_limit_bytes=48 << 20),
        name="conv_outer",
    )(weights, bias, coef, *state, xlo, xhi, clo, chi, volume)


def shift(array, axis, by):
    size = lax.axis_size(axis)
    pairs = [(i, i + by) for i in range(size) if 0 <= i + by < size]
    return lax.ppermute(array, axis, pairs)


def on_device(
    tile_pixel, tile_voxel, tile_count, features, interp, conv_weight, conv_bias, smooth_coef
):
    feats = features[0, 0]
    tiles = interp[0, 0]
    packed, weights, bias = partials(
        tile_pixel[0, 0],
        tile_voxel[0, 0],
        tile_count[0],
        feats,
        conv_weight.reshape(27, C, C),
        conv_bias[None],
        tiles,
    )
    got = lax.all_to_all(packed, ("views", "bricks"), split_axis=0, concat_axis=0, tiled=True)
    main, lo, hi, ylo, yhi = lift(got)
    from_low = shift(yhi, "views", 1)
    from_high = shift(ylo, "views", -1)
    xlo = shift(hi, "bricks", 1)
    xhi = shift(lo, "bricks", -1)
    clo = shift(jnp.stack([from_low[BX - 2 :], from_high[BX - 2 :]]), "bricks", 1)
    chi = shift(jnp.stack([from_low[:2], from_high[:2]]), "bricks", -1)
    volume, *state = conv_inner(weights, bias, smooth_coef, main, from_low, from_high)
    return conv_outer(weights, bias, smooth_coef, state, xlo, xhi, clo, chi, volume)


def solution(mesh):
    in_specs = (
        P("views", "bricks", None),
        P("views", "bricks", None),
        P("views", "bricks"),
        P("views", "bricks", None, None, None),
        P("views", "bricks", None, None, None),
        P(),
        P(),
        P("bricks", "views", None),
    )
    out_specs = P(None, "bricks", "views", None)
    return jax.shard_map(
        on_device, mesh=mesh, in_specs=in_specs, out_specs=out_specs, check_vma=False
    )
```

```python
import functools

import jax
import jax.numpy as jnp
from jax import lax
from jax.experimental import pallas as pl
from jax.experimental.pallas import tpu as pltpu
from jax.sharding import PartitionSpec as P

C = 64
PIX = 128
Z = 128
BX = 8
BY = 32
BLK = 64
VOXB = 512
ROW = BY * Z
WIDE = (BY + 4) * Z
GATED = (BY + 2) * Z
SEND = 16
LIMIT = 32
PACK = 4 * C + 8
PITCH = 40


def partial_kernel(
    pixel_ref, voxel_ref, count_ref, feats_ref, cw_ref, cb_ref, tiles_ref,
    out_ref, w_ref, bias_ref,
    tiles, out, feats, cw, sems, done, small,
):
    chunks = tiles.shape[0] // SEND

    def load(k):
        rows = pl.ds(pl.multiple_of(k * SEND, SEND), SEND)
        return pltpu.make_async_copy(tiles_ref.at[rows], tiles.at[rows], sems.at[k])

    def store(k):
        rows = pl.ds(pl.multiple_of(k * SEND, SEND), SEND)
        return pltpu.make_async_copy(out.at[rows], out_ref.at[rows], done.at[k])

    early = [
        pltpu.make_async_copy(cw_ref, cw, small.at[0]),
        pltpu.make_async_copy(feats_ref, feats, small.at[1]),
    ]
    for copy in early:
        copy.start()
    for k in range(chunks):
        load(k).start()
    for copy in early:
        copy.wait()

    taps = 9
    for dx in range(3):
        for q in range(0, taps, 2):
            pieces = [cw[dx * taps + r] for r in range(q, min(q + 2, taps))]
            both = pieces[0] if len(pieces) == 1 else jnp.concatenate(pieces, axis=1)
            w_ref[dx * C : (dx + 1) * C, q * C : q * C + both.shape[1]] = both
    eye = lax.broadcasted_iota(jnp.int32, (C, C), 0) == lax.broadcasted_iota(jnp.int32, (C, C), 1)
    column = jnp.where(eye, jnp.broadcast_to(cb_ref[...], (C, C)), 0.0)
    bias_ref[...] = jnp.broadcast_to(jnp.sum(column, axis=1, keepdims=True), (C, 2 * Z))
    me = lax.axis_index("views") * lax.axis_size("bricks") + lax.axis_index("bricks")
    slots = tiles.shape[0]
    offset = lax.rem(me * 37, slots)
    count = count_ref[0]

    def chunk(k, carry):
        load(k).wait()
        for i in range(SEND):
            slot = k * SEND + i
            p = jnp.dot(
                feats[pixel_ref[slot]], tiles[slot], preferred_element_type=jnp.float32
            )
            for q in range(4):
                out[slot, q * C : (q + 1) * C, :] = p[:, q * Z : (q + 1) * Z].astype(jnp.bfloat16)
            place = slot - offset
            place = jnp.where(place < 0, place + slots, place)
            target = jnp.where(place < count, voxel_ref[slot], BLK)
            block = jnp.full((PACK - 4 * C, Z), target.astype(jnp.float32), jnp.float32)
            out[slot, 4 * C : PACK, :] = block.astype(jnp.bfloat16)
        store(k).start()
        return carry

    lax.fori_loop(0, chunks, chunk, 0)
    for k in range(chunks):
        store(k).wait()


def partials(pixel_ids, voxel_ids, count, feats, conv_weight, conv_bias, tiles):
    n = tiles.shape[0]
    smem = pl.BlockSpec(memory_space=pltpu.SMEM)
    vmem = pl.BlockSpec(memory_space=pltpu.VMEM)
    hbm = pl.BlockSpec(memory_space=pl.ANY)
    return pl.pallas_call(
        partial_kernel,
        in_specs=[smem, smem, smem, hbm, hbm, vmem, hbm],
        out_specs=[hbm, vmem, vmem],
        scratch_shapes=[
            pltpu.VMEM((n, PIX, VOXB), jnp.bfloat16),
            pltpu.VMEM((n, PACK, Z), jnp.bfloat16),
            pltpu.VMEM(feats.shape, jnp.bfloat16),
            pltpu.VMEM(conv_weight.shape, jnp.bfloat16),
            pltpu.SemaphoreType.DMA((n // SEND,)),
            pltpu.SemaphoreType.DMA((n // SEND,)),
            pltpu.SemaphoreType.DMA((2,)),
        ],
        out_shape=[
            jax.ShapeDtypeStruct((n, PACK, Z), jnp.bfloat16),
            jax.ShapeDtypeStruct((3 * C, 9 * C), jnp.bfloat16),
            jax.ShapeDtypeStruct((C, 2 * Z), jnp.float32),
        ],
        compiler_params=pltpu.CompilerParams(vmem_limit_bytes=48 << 20),
        name="partials",
    )(pixel_ids, voxel_ids, count, feats, conv_weight, conv_bias, tiles)


def lift_kernel(
    part_ref, main_ref, lo_ref, hi_ref, ylo_ref, yhi_ref, ll_ref, lh_ref, hl_ref, hh_ref,
    acc, ids, tgt_ref, sem,
):
    n = part_ref.shape[0]
    lane = lax.broadcasted_iota(jnp.int32, (8, Z), 1)
    table = jnp.zeros((8, Z), jnp.float32)
    for i in range(n):
        table = jnp.where(lane == i, part_ref[i, 4 * C : PACK].astype(jnp.float32), table)
    ids[...] = table.astype(jnp.int32)
    move = pltpu.make_async_copy(ids, tgt_ref, sem)
    move.start()
    acc[...] = jnp.zeros_like(acc)
    move.wait()

    def add(i, carry):
        block = tgt_ref[0, i]

        @pl.when(block < BLK)
        def _():
            acc[block] = acc[block] + part_ref[i, : 4 * C].astype(jnp.float32)

        return carry

    lax.fori_loop(0, n, add, 0)

    for x in range(BX):
        for y in range(BY):
            v = acc[x * (BY // 4) + y // 4, (y % 4) * C : (y % 4 + 1) * C, :]
            v = jnp.maximum(v, 0.0).astype(jnp.bfloat16)
            cols = slice(y * Z, (y + 1) * Z)
            main_ref[x, :, cols] = v
            if x < 2:
                lo_ref[x, :, cols] = v
            if x >= BX - 2:
                hi_ref[x - BX + 2, :, cols] = v
            for inside_y, first, face, low, high in (
                (y < 2, 0, ylo_ref, ll_ref, hl_ref),
                (y >= BY - 2, BY - 2, yhi_ref, lh_ref, hh_ref),
            ):
                if inside_y:
                    strip = slice((y - first) * Z, (y - first + 1) * Z)
                    face[x, :, strip] = v
                    if x < 2:
                        low[x, :, strip] = v
                    if x >= BX - 2:
                        high[x - BX + 2, :, strip] = v


def lift(part):
    vmem = pl.BlockSpec(memory_space=pltpu.VMEM)
    return pl.pallas_call(
        lift_kernel,
        in_specs=[vmem],
        out_specs=[vmem] * 9,
        scratch_shapes=[
            pltpu.VMEM((BLK, 4 * C, Z), jnp.float32),
            pltpu.VMEM((8, Z), jnp.int32),
            pltpu.SMEM((8, Z), jnp.int32),
            pltpu.SemaphoreType.DMA,
        ],
        out_shape=[
            jax.ShapeDtypeStruct((BX, C, ROW), jnp.bfloat16),
            jax.ShapeDtypeStruct((2, C, ROW), jnp.bfloat16),
            jax.ShapeDtypeStruct((2, C, ROW), jnp.bfloat16),
            jax.ShapeDtypeStruct((BX, C, 2 * Z), jnp.bfloat16),
            jax.ShapeDtypeStruct((BX, C, 2 * Z), jnp.bfloat16),
        ]
        + [jax.ShapeDtypeStruct((2, C, 2 * Z), jnp.bfloat16)] * 4,
        compiler_params=pltpu.CompilerParams(vmem_limit_bytes=32 << 20),
        name="lift",
    )(part)


def inside():
    brick, view = lax.axis_index("bricks"), lax.axis_index("views")
    return [
        jnp.where(test, 1.0, 0.0).astype(jnp.float32)
        for test in (
            brick > 0,
            brick < lax.axis_size("bricks") - 1,
            view > 0,
            view < lax.axis_size("views") - 1,
        )
    ]


def shifted(v, first, last):
    down = jnp.where(first, 0.0, pltpu.roll(v, 1, 1))
    up = jnp.where(last, 0.0, pltpu.roll(v, Z - 1, 1))
    return down, up


def edges():
    lane = lax.broadcasted_iota(jnp.int32, (C, Z), 1)
    return lane == 0, lane == Z - 1


def stage(pieces, xs, y, ends):
    cols = slice(y * Z, (y + 1) * Z)
    left, mid, right = pieces
    if y < 2:
        v = left[:, y * Z : (y + 1) * Z]
    elif y < BY + 2:
        v = mid[:, (y - 2) * Z : (y - 1) * Z]
    else:
        v = right[:, (y - BY - 2) * Z : (y - BY - 1) * Z]
    down, up = shifted(v.astype(jnp.float32), *ends)
    xs[0:C, cols] = down.astype(jnp.bfloat16)
    xs[C : 2 * C, cols] = v
    xs[2 * C : 3 * C, cols] = up.astype(jnp.bfloat16)


def stage_rows(t):
    return range(2 * t, 2 * t + 2 if t < BY // 2 else BY + 4)


def window(xs, t):
    return jnp.concatenate(
        [xs[:, (t * 2 + dy) * Z : (t * 2 + dy + 2) * Z] for dy in range(3)], axis=0
    )


def split_rows(g, t, flags):
    rows = [g[:, :Z], g[:, Z:]]
    if t == 0:
        rows[0] = rows[0] * flags[2]
    if t == BY // 2:
        rows[1] = rows[1] * flags[3]
    return rows


def inner_kernel(
    w_ref, bias_ref, coef_ref, main_ref, ylo_ref, yhi_ref,
    out_ref, outer_ref, edge_ref, near_ref, pend_ref,
    xs_a, xs_b, acc_a, acc_b, prev, pend, flat_a, flat_b, packed, done,
):
    ends, flags = edges(), inside()
    pieces = [(ylo_ref.at[x], main_ref.at[x], yhi_ref.at[x]) for x in range(BX)]
    stores = [
        pltpu.make_async_copy(packed.at[k], out_ref.at[:, k + 2], done.at[k])
        for k in range(BX - 4)
    ]
    bias = bias_ref[...]
    weights = w_ref[...]
    buffers, flats = (xs_a, xs_b), (flat_a, flat_b)
    for y in range(BY + 4):
        stage(pieces[0], xs_a, y, ends)
    for x in range(BX):
        xs, xs_next, flat = buffers[x % 2], buffers[(x + 1) % 2], flats[x % 2]
        new = x - 1
        before = None
        for t in range((BY + 2) // 2):
            if x + 1 < BX:
                for y in stage_rows(t):
                    stage(pieces[x + 1], xs_next, y, ends)
            cols = slice(t * 2 * Z, (t + 1) * 2 * Z)
            p = jnp.dot(weights, window(xs, t), preferred_element_type=jnp.float32)
            if x == 0:
                outer_ref[0, :, cols] = p[2 * C :]
                acc_b[:, cols] = p[C : 2 * C]
                acc_a[:, cols] = p[:C]
                continue
            total = acc_b[:, cols] + p[2 * C :]
            if x == BX - 1:
                edge_ref[1, :, cols] = acc_a[:, cols] + p[C : 2 * C]
                outer_ref[1, :, cols] = p[:C]
            else:
                acc_b[:, cols] = acc_a[:, cols] + p[C : 2 * C]
                acc_a[:, cols] = p[:C]
            if x == 1:
                edge_ref[0, :, cols] = total
                continue
            rows = split_rows(jnp.maximum(total + bias, 0.0), t, flags)
            if t > 0:
                four = before + rows
                for k in range(2):
                    y = 2 * t - 2 + k
                    here = slice(y * Z, (y + 1) * Z)
                    low, mid, high = four[k], four[k + 1], four[k + 2]
                    down, up = shifted(mid, *ends)
                    beside = low + high + down + up
                    if new > 1:
                        beside = beside + prev[:, here]
                        full = pend[:, here] + coef_ref[new - 1, y : y + 1, :] * mid
                        if new == 2:
                            pend_ref[0, :, here] = full
                        else:
                            flat[pl.ds(y, C, stride=PITCH), :] = full
                    later = mid + coef_ref[new, y : y + 1, :] * (beside - 6.0 * mid)
                    if new == 1:
                        near_ref[0, :, here] = mid
                    if new == BX - 2:
                        near_ref[1, :, here] = mid
                        pend_ref[1, :, here] = later
                    else:
                        prev[:, here] = mid
                        pend[:, here] = later
            before = rows
        if new > 2:
            packed[new - 3] = flat[...].reshape(C, PITCH, Z)[:, :BY].astype(jnp.bfloat16)
            stores[new - 3].start()
    for copy in stores:
        copy.wait()


def outer_kernel(
    w_ref, bias_ref, coef_ref, outer_ref, edge_ref, near_ref, pend_ref,
    xlo_ref, xhi_ref, ll_ref, lh_ref, hl_ref, hh_ref, part_ref,
    out_ref,
    xs_0, xs_1, xs_2, xs_3, flat_a, flat_b, packed, done,
):
    ends, flags = edges(), inside()
    pieces = [
        (left.at[q], face.at[q], right.at[q])
        for left, face, right, q in (
            (ll_ref, xlo_ref, lh_ref, 0),
            (ll_ref, xlo_ref, lh_ref, 1),
            (hl_ref, xhi_ref, hh_ref, 1),
            (hl_ref, xhi_ref, hh_ref, 0),
        )
    ]
    targets = [(0, 1), (BX - 1, BX - 2)]
    stores = [
        [
            pltpu.make_async_copy(packed.at[2 * s + k], out_ref.at[:, targets[s][k]], done.at[s, k])
            for k in range(2)
        ]
        for s in range(2)
    ]
    bias = bias_ref[...]
    planes = (xs_0, xs_1, xs_2, xs_3)
    for p in range(2):
        for y in range(BY + 4):
            stage(pieces[p], planes[p], y, ends)
    for s in range(2):
        far, nearer = planes[2 * s], planes[2 * s + 1]
        w_side = w_ref[2 * s * C : (2 * s + 1) * C]
        w_both = jnp.concatenate([w_ref[C : 2 * C], w_side], axis=0)
        e, i = targets[s]
        before = None
        for t in range((BY + 2) // 2):
            if s == 0:
                for p in (2, 3):
                    for y in stage_rows(t):
                        stage(pieces[p], planes[p], y, ends)
            cols = slice(t * 2 * Z, (t + 1) * 2 * Z)
            a = jnp.dot(w_side, window(far, t), preferred_element_type=jnp.float32)
            b = jnp.dot(w_both, window(nearer, t), preferred_element_type=jnp.float32)
            past = jnp.maximum(outer_ref[s, :, cols] + a + b[:C] + bias, 0.0) * flags[s]
            rows = split_rows(
                jnp.maximum(edge_ref[s, :, cols] + b[C:] + bias, 0.0), t, flags
            )
            past = [past[:, :Z], past[:, Z:]]
            if t > 0:
                four = before[0] + rows
                two = [before[1][1], past[0]]
                for k in range(2):
                    y = 2 * t - 2 + k
                    here = slice(y * Z, (y + 1) * Z)
                    low, mid, high = four[k], four[k + 1], four[k + 2]
                    down, up = shifted(mid, *ends)
                    beside = low + high + down + up + two[k] + near_ref[s, :, here]
                    flat_a[pl.ds(y, C, stride=PITCH), :] = mid + coef_ref[e, y : y + 1, :] * (
                        beside - 6.0 * mid
                    )
                    flat_b[pl.ds(y, C, stride=PITCH), :] = (
                        pend_ref[s, :, here] + coef_ref[i, y : y + 1, :] * mid
                    )
            before = (rows, past)
        for k, flat in enumerate((flat_a, flat_b)):
            packed[2 * s + k] = flat[...].reshape(C, PITCH, Z)[:, :BY].astype(jnp.bfloat16)
            stores[s][k].start()
    for group in stores:
        for copy in group:
            copy.wait()


def conv_inner(weights, bias, coef, main, ylo, yhi):
    hbm = pl.BlockSpec(memory_space=pl.ANY)
    vmem = pl.BlockSpec(memory_space=pltpu.VMEM)
    state = lambda width: jax.ShapeDtypeStruct((2, C, width), jnp.float32)
    return pl.pallas_call(
        inner_kernel,
        in_specs=[vmem] * 6,
        out_specs=[hbm] + [vmem] * 4,
        scratch_shapes=[
            pltpu.VMEM((3 * C, WIDE), jnp.bfloat16),
            pltpu.VMEM((3 * C, WIDE), jnp.bfloat16),
            pltpu.VMEM((C, GATED), jnp.float32),
            pltpu.VMEM((C, GATED), jnp.float32),
            pltpu.VMEM((C, ROW), jnp.float32),
            pltpu.VMEM((C, ROW), jnp.float32),
            pltpu.VMEM((C * PITCH, Z), jnp.float32),
            pltpu.VMEM((C * PITCH, Z), jnp.float32),
            pltpu.VMEM((BX - 4, C, BY, Z), jnp.bfloat16),
            pltpu.SemaphoreType.DMA((BX - 4,)),
        ],
        out_shape=[
            jax.ShapeDtypeStruct((C, BX, BY, Z), jnp.bfloat16),
            state(GATED),
            state(GATED),
            state(ROW),
            state(ROW),
        ],
        compiler_params=pltpu.CompilerParams(vmem_limit_bytes=LIMIT << 20),
        name="conv_inner",
    )(weights, bias, coef, main, ylo, yhi)


def conv_outer(weights, bias, coef, state, faces, corners, volume):
    hbm = pl.BlockSpec(memory_space=pl.ANY)
    vmem = pl.BlockSpec(memory_space=pltpu.VMEM)
    return pl.pallas_call(
        outer_kernel,
        in_specs=[vmem] * 13 + [hbm],
        out_specs=hbm,
        scratch_shapes=[pltpu.VMEM((3 * C, WIDE), jnp.bfloat16)] * 4
        + [pltpu.VMEM((C * PITCH, Z), jnp.float32)] * 2
        + [
            pltpu.VMEM((4, C, BY, Z), jnp.bfloat16),
            pltpu.SemaphoreType.DMA((2, 2)),
        ],
        out_shape=jax.ShapeDtypeStruct((C, BX, BY, Z), jnp.bfloat16),
        input_output_aliases={13: 0},
        compiler_params=pltpu.CompilerParams(vmem_limit_bytes=LIMIT << 20),
        name="conv_outer",
    )(weights, bias, coef, *state, *faces, *corners, volume)


def shift(array, along_y, along_x):
    views, bricks = lax.axis_size("views"), lax.axis_size("bricks")
    pairs = [
        (v * bricks + b, (v + along_y) * bricks + b + along_x)
        for v in range(views)
        for b in range(bricks)
        if 0 <= v + along_y < views and 0 <= b + along_x < bricks
    ]
    return lax.ppermute(array, ("views", "bricks"), pairs)


def on_device(
    tile_pixel, tile_voxel, tile_count, features, interp, conv_weight, conv_bias, smooth_coef
):
    feats = features[0, 0]
    tiles = interp[0, 0]
    packed, weights, bias = partials(
        tile_pixel[0, 0],
        tile_voxel[0, 0],
        tile_count[0],
        feats,
        conv_weight.reshape(27, C, C),
        conv_bias[None],
        tiles,
    )
    got = lax.all_to_all(packed, ("views", "bricks"), split_axis=0, concat_axis=0, tiled=True)
    main, lo, hi, ylo, yhi, ll, lh, hl, hh = lift(got)
    from_low = shift(yhi, 1, 0)
    from_high = shift(ylo, -1, 0)
    faces = shift(hi, 0, 1), shift(lo, 0, -1)
    corners = shift(hh, 1, 1), shift(hl, -1, 1), shift(lh, 1, -1), shift(ll, -1, -1)
    volume, *state = conv_inner(weights, bias, smooth_coef, main, from_low, from_high)
    return conv_outer(weights, bias, smooth_coef, state, faces, corners, volume)


def solution(mesh):
    in_specs = (
        P("views", "bricks", None),
        P("views", "bricks", None),
        P("views", "bricks"),
        P("views", "bricks", None, None, None),
        P("views", "bricks", None, None, None),
        P(),
        P(),
        P("bricks", "views", None),
    )
    out_specs = P(None, "bricks", "views", None)
    return jax.shard_map(
        on_device, mesh=mesh, in_specs=in_specs, out_specs=out_specs, check_vma=False
    )
```

```python
import functools

import jax
import jax.numpy as jnp
from jax import lax
from jax.experimental import pallas as pl
from jax.experimental.pallas import tpu as pltpu
from jax.sharding import PartitionSpec as P

C = 64
PIX = 128
Z = 128
BX = 8
BY = 32
BLK = 64
VOXB = 512
ROW = BY * Z
WIDE = (BY + 4) * Z
GATED = (BY + 2) * Z
SEND = 16
LIMIT = 32
PACK = 4 * C + 8
PITCH = 40


def partial_kernel(
    pixel_ref, voxel_ref, count_ref, feats_ref, cw_ref, cb_ref, tiles_ref,
    out_ref, w_ref, bias_ref,
    tiles, out, feats, cw, sems, done, small,
):
    chunks = tiles.shape[0] // SEND

    def load(k):
        rows = pl.ds(pl.multiple_of(k * SEND, SEND), SEND)
        return pltpu.make_async_copy(tiles_ref.at[rows], tiles.at[rows], sems.at[k])

    def store(k):
        rows = pl.ds(pl.multiple_of(k * SEND, SEND), SEND)
        return pltpu.make_async_copy(out.at[rows], out_ref.at[rows], done.at[k])

    early = [
        pltpu.make_async_copy(cw_ref, cw, small.at[0]),
        pltpu.make_async_copy(feats_ref, feats, small.at[1]),
    ]
    for copy in early:
        copy.start()
    for k in range(chunks):
        load(k).start()
    for copy in early:
        copy.wait()

    taps = 9
    for dx in range(3):
        for q in range(0, taps, 2):
            pieces = [cw[dx * taps + r] for r in range(q, min(q + 2, taps))]
            both = pieces[0] if len(pieces) == 1 else jnp.concatenate(pieces, axis=1)
            w_ref[dx * C : (dx + 1) * C, q * C : q * C + both.shape[1]] = both
    eye = lax.broadcasted_iota(jnp.int32, (C, C), 0) == lax.broadcasted_iota(jnp.int32, (C, C), 1)
    column = jnp.where(eye, jnp.broadcast_to(cb_ref[...], (C, C)), 0.0)
    bias_ref[...] = jnp.broadcast_to(jnp.sum(column, axis=1, keepdims=True), (C, 2 * Z))
    me = lax.axis_index("views") * lax.axis_size("bricks") + lax.axis_index("bricks")
    slots = tiles.shape[0]
    offset = lax.rem(me * 37, slots)
    count = count_ref[0]

    def chunk(k, carry):
        load(k).wait()
        for i in range(SEND):
            slot = k * SEND + i
            p = jnp.dot(
                feats[pixel_ref[slot]], tiles[slot], preferred_element_type=jnp.float32
            )
            for q in range(4):
                out[slot, q * C : (q + 1) * C, :] = p[:, q * Z : (q + 1) * Z].astype(jnp.bfloat16)
            place = slot - offset
            place = jnp.where(place < 0, place + slots, place)
            target = jnp.where(place < count, voxel_ref[slot], BLK)
            block = jnp.full((PACK - 4 * C, Z), target.astype(jnp.float32), jnp.float32)
            out[slot, 4 * C : PACK, :] = block.astype(jnp.bfloat16)
        store(k).start()
        return carry

    lax.fori_loop(0, chunks, chunk, 0)
    for k in range(chunks):
        store(k).wait()


def partials(pixel_ids, voxel_ids, count, feats, conv_weight, conv_bias, tiles):
    n = tiles.shape[0]
    smem = pl.BlockSpec(memory_space=pltpu.SMEM)
    vmem = pl.BlockSpec(memory_space=pltpu.VMEM)
    hbm = pl.BlockSpec(memory_space=pl.ANY)
    return pl.pallas_call(
        partial_kernel,
        in_specs=[smem, smem, smem, hbm, hbm, vmem, hbm],
        out_specs=[hbm, vmem, vmem],
        scratch_shapes=[
            pltpu.VMEM((n, PIX, VOXB), jnp.bfloat16),
            pltpu.VMEM((n, PACK, Z), jnp.bfloat16),
            pltpu.VMEM(feats.shape, jnp.bfloat16),
            pltpu.VMEM(conv_weight.shape, jnp.bfloat16),
            pltpu.SemaphoreType.DMA((n // SEND,)),
            pltpu.SemaphoreType.DMA((n // SEND,)),
            pltpu.SemaphoreType.DMA((2,)),
        ],
        out_shape=[
            jax.ShapeDtypeStruct((n, PACK, Z), jnp.bfloat16),
            jax.ShapeDtypeStruct((3 * C, 9 * C), jnp.bfloat16),
            jax.ShapeDtypeStruct((C, 2 * Z), jnp.float32),
        ],
        compiler_params=pltpu.CompilerParams(vmem_limit_bytes=48 << 20),
        name="partials",
    )(pixel_ids, voxel_ids, count, feats, conv_weight, conv_bias, tiles)


def lift_kernel(
    part_ref, main_ref, lo_ref, hi_ref, ylo_ref, yhi_ref,
    acc, ids, tgt_ref, sem,
):
    n = part_ref.shape[0]
    lane = lax.broadcasted_iota(jnp.int32, (8, Z), 1)
    table = jnp.zeros((8, Z), jnp.float32)
    for i in range(n):
        table = jnp.where(lane == i, part_ref[i, 4 * C : PACK].astype(jnp.float32), table)
    ids[...] = table.astype(jnp.int32)
    move = pltpu.make_async_copy(ids, tgt_ref, sem)
    move.start()
    acc[...] = jnp.zeros_like(acc)
    move.wait()

    def add(i, carry):
        block = tgt_ref[0, i]

        @pl.when(block < BLK)
        def _():
            acc[block] = acc[block] + part_ref[i, : 4 * C].astype(jnp.float32)

        return carry

    lax.fori_loop(0, n, add, 0)

    for x in range(BX):
        for y in range(BY):
            v = acc[x * (BY // 4) + y // 4, (y % 4) * C : (y % 4 + 1) * C, :]
            v = jnp.maximum(v, 0.0).astype(jnp.bfloat16)
            cols = slice(y * Z, (y + 1) * Z)
            main_ref[x, :, cols] = v
            if x < 2:
                lo_ref[x, :, cols] = v
            if x >= BX - 2:
                hi_ref[x - BX + 2, :, cols] = v
            if y < 2:
                ylo_ref[x, :, cols] = v
            if y >= BY - 2:
                yhi_ref[x, :, (y - BY + 2) * Z : (y - BY + 3) * Z] = v


def lift(part):
    vmem = pl.BlockSpec(memory_space=pltpu.VMEM)
    return pl.pallas_call(
        lift_kernel,
        in_specs=[vmem],
        out_specs=[vmem] * 5,
        scratch_shapes=[
            pltpu.VMEM((BLK, 4 * C, Z), jnp.float32),
            pltpu.VMEM((8, Z), jnp.int32),
            pltpu.SMEM((8, Z), jnp.int32),
            pltpu.SemaphoreType.DMA,
        ],
        out_shape=[
            jax.ShapeDtypeStruct((BX, C, ROW), jnp.bfloat16),
            jax.ShapeDtypeStruct((2, C, ROW), jnp.bfloat16),
            jax.ShapeDtypeStruct((2, C, ROW), jnp.bfloat16),
            jax.ShapeDtypeStruct((BX, C, 2 * Z), jnp.bfloat16),
            jax.ShapeDtypeStruct((BX, C, 2 * Z), jnp.bfloat16),
        ],
        compiler_params=pltpu.CompilerParams(vmem_limit_bytes=32 << 20),
        name="lift",
    )(part)


def inside():
    brick, view = lax.axis_index("bricks"), lax.axis_index("views")
    return [
        jnp.where(test, 1.0, 0.0).astype(jnp.float32)
        for test in (
            brick > 0,
            brick < lax.axis_size("bricks") - 1,
            view > 0,
            view < lax.axis_size("views") - 1,
        )
    ]


def shifted(v, first, last):
    down = jnp.where(first, 0.0, pltpu.roll(v, 1, 1))
    up = jnp.where(last, 0.0, pltpu.roll(v, Z - 1, 1))
    return down, up


def edges():
    lane = lax.broadcasted_iota(jnp.int32, (C, Z), 1)
    return lane == 0, lane == Z - 1


def stage(pieces, xs, y, ends):
    cols = slice(y * Z, (y + 1) * Z)
    left, mid, right = pieces
    if y < 2:
        v = left[:, y * Z : (y + 1) * Z]
    elif y < BY + 2:
        v = mid[:, (y - 2) * Z : (y - 1) * Z]
    else:
        v = right[:, (y - BY - 2) * Z : (y - BY - 1) * Z]
    down, up = shifted(v.astype(jnp.float32), *ends)
    xs[0:C, cols] = down.astype(jnp.bfloat16)
    xs[C : 2 * C, cols] = v
    xs[2 * C : 3 * C, cols] = up.astype(jnp.bfloat16)


def stage_rows(t):
    return range(2 * t, 2 * t + 2 if t < BY // 2 else BY + 4)


def window(xs, t):
    return jnp.concatenate(
        [xs[:, (t * 2 + dy) * Z : (t * 2 + dy + 2) * Z] for dy in range(3)], axis=0
    )


def split_rows(g, t, flags):
    rows = [g[:, :Z], g[:, Z:]]
    if t == 0:
        rows[0] = rows[0] * flags[2]
    if t == BY // 2:
        rows[1] = rows[1] * flags[3]
    return rows


def inner_kernel(
    w_ref, bias_ref, coef_ref, main_ref, ylo_ref, yhi_ref,
    out_ref, outer_ref, edge_ref, near_ref, pend_ref,
    xs_a, xs_b, acc_a, acc_b, prev, pend, flat_a, flat_b, packed, done,
):
    ends, flags = edges(), inside()
    pieces = [(ylo_ref.at[x], main_ref.at[x], yhi_ref.at[x]) for x in range(BX)]
    stores = [
        pltpu.make_async_copy(packed.at[k], out_ref.at[:, k + 2], done.at[k])
        for k in range(BX - 4)
    ]
    bias = bias_ref[...]
    weights = w_ref[...]
    buffers, flats = (xs_a, xs_b), (flat_a, flat_b)
    for y in range(BY + 4):
        stage(pieces[0], xs_a, y, ends)
    for x in range(BX):
        xs, xs_next, flat = buffers[x % 2], buffers[(x + 1) % 2], flats[x % 2]
        new = x - 1
        before = None
        for t in range((BY + 2) // 2):
            if x + 1 < BX:
                for y in stage_rows(t):
                    stage(pieces[x + 1], xs_next, y, ends)
            cols = slice(t * 2 * Z, (t + 1) * 2 * Z)
            p = jnp.dot(weights, window(xs, t), preferred_element_type=jnp.float32)
            if x == 0:
                outer_ref[0, :, cols] = p[2 * C :]
                acc_b[:, cols] = p[C : 2 * C]
                acc_a[:, cols] = p[:C]
                continue
            total = acc_b[:, cols] + p[2 * C :]
            if x == BX - 1:
                edge_ref[1, :, cols] = acc_a[:, cols] + p[C : 2 * C]
                outer_ref[1, :, cols] = p[:C]
            else:
                acc_b[:, cols] = acc_a[:, cols] + p[C : 2 * C]
                acc_a[:, cols] = p[:C]
            if x == 1:
                edge_ref[0, :, cols] = total
                continue
            rows = split_rows(jnp.maximum(total + bias, 0.0), t, flags)
            if t > 0:
                four = before + rows
                for k in range(2):
                    y = 2 * t - 2 + k
                    here = slice(y * Z, (y + 1) * Z)
                    low, mid, high = four[k], four[k + 1], four[k + 2]
                    down, up = shifted(mid, *ends)
                    beside = low + high + down + up
                    if new > 1:
                        beside = beside + prev[:, here]
                        full = pend[:, here] + coef_ref[new - 1, y : y + 1, :] * mid
                        if new == 2:
                            pend_ref[0, :, here] = full
                        else:
                            flat[pl.ds(y, C, stride=PITCH), :] = full
                    later = mid + coef_ref[new, y : y + 1, :] * (beside - 6.0 * mid)
                    if new == 1:
                        near_ref[0, :, here] = mid
                    if new == BX - 2:
                        near_ref[1, :, here] = mid
                        pend_ref[1, :, here] = later
                    else:
                        prev[:, here] = mid
                        pend[:, here] = later
            before = rows
        if new > 2:
            packed[new - 3] = flat[...].reshape(C, PITCH, Z)[:, :BY].astype(jnp.bfloat16)
            stores[new - 3].start()
    for copy in stores:
        copy.wait()


def outer_kernel(
    w_ref, bias_ref, coef_ref, outer_ref, edge_ref, near_ref, pend_ref,
    xlo_ref, xhi_ref, clo_ref, chi_ref, part_ref,
    out_ref,
    xs_0, xs_1, xs_2, xs_3, flat_a, flat_b, packed, done,
):
    ends, flags = edges(), inside()
    pieces = [
        (corner.at[0, q], face.at[q], corner.at[1, q])
        for face, corner, q in (
            (xlo_ref, clo_ref, 0),
            (xlo_ref, clo_ref, 1),
            (xhi_ref, chi_ref, 1),
            (xhi_ref, chi_ref, 0),
        )
    ]
    targets = [(0, 1), (BX - 1, BX - 2)]
    stores = [
        [
            pltpu.make_async_copy(packed.at[2 * s + k], out_ref.at[:, targets[s][k]], done.at[s, k])
            for k in range(2)
        ]
        for s in range(2)
    ]
    bias = bias_ref[...]
    planes = (xs_0, xs_1, xs_2, xs_3)
    for p in range(2):
        for y in range(BY + 4):
            stage(pieces[p], planes[p], y, ends)
    for s in range(2):
        far, nearer = planes[2 * s], planes[2 * s + 1]
        w_side = w_ref[2 * s * C : (2 * s + 1) * C]
        w_both = jnp.concatenate([w_ref[C : 2 * C], w_side], axis=0)
        e, i = targets[s]
        before = None
        for t in range((BY + 2) // 2):
            if s == 0:
                for p in (2, 3):
                    for y in stage_rows(t):
                        stage(pieces[p], planes[p], y, ends)
            cols = slice(t * 2 * Z, (t + 1) * 2 * Z)
            a = jnp.dot(w_side, window(far, t), preferred_element_type=jnp.float32)
            b = jnp.dot(w_both, window(nearer, t), preferred_element_type=jnp.float32)
            past = jnp.maximum(outer_ref[s, :, cols] + a + b[:C] + bias, 0.0) * flags[s]
            rows = split_rows(
                jnp.maximum(edge_ref[s, :, cols] + b[C:] + bias, 0.0), t, flags
            )
            past = [past[:, :Z], past[:, Z:]]
            if t > 0:
                four = before[0] + rows
                two = [before[1][1], past[0]]
                for k in range(2):
                    y = 2 * t - 2 + k
                    here = slice(y * Z, (y + 1) * Z)
                    low, mid, high = four[k], four[k + 1], four[k + 2]
                    down, up = shifted(mid, *ends)
                    beside = low + high + down + up + two[k] + near_ref[s, :, here]
                    flat_a[pl.ds(y, C, stride=PITCH), :] = mid + coef_ref[e, y : y + 1, :] * (
                        beside - 6.0 * mid
                    )
                    flat_b[pl.ds(y, C, stride=PITCH), :] = (
                        pend_ref[s, :, here] + coef_ref[i, y : y + 1, :] * mid
                    )
            before = (rows, past)
        for k, flat in enumerate((flat_a, flat_b)):
            packed[2 * s + k] = flat[...].reshape(C, PITCH, Z)[:, :BY].astype(jnp.bfloat16)
            stores[s][k].start()
    for group in stores:
        for copy in group:
            copy.wait()


def conv_inner(weights, bias, coef, main, ylo, yhi):
    hbm = pl.BlockSpec(memory_space=pl.ANY)
    vmem = pl.BlockSpec(memory_space=pltpu.VMEM)
    state = lambda width: jax.ShapeDtypeStruct((2, C, width), jnp.float32)
    return pl.pallas_call(
        inner_kernel,
        in_specs=[vmem] * 6,
        out_specs=[hbm] + [vmem] * 4,
        scratch_shapes=[
            pltpu.VMEM((3 * C, WIDE), jnp.bfloat16),
            pltpu.VMEM((3 * C, WIDE), jnp.bfloat16),
            pltpu.VMEM((C, GATED), jnp.float32),
            pltpu.VMEM((C, GATED), jnp.float32),
            pltpu.VMEM((C, ROW), jnp.float32),
            pltpu.VMEM((C, ROW), jnp.float32),
            pltpu.VMEM((C * PITCH, Z), jnp.float32),
            pltpu.VMEM((C * PITCH, Z), jnp.float32),
            pltpu.VMEM((BX - 4, C, BY, Z), jnp.bfloat16),
            pltpu.SemaphoreType.DMA((BX - 4,)),
        ],
        out_shape=[
            jax.ShapeDtypeStruct((C, BX, BY, Z), jnp.bfloat16),
            state(GATED),
            state(GATED),
            state(ROW),
            state(ROW),
        ],
        compiler_params=pltpu.CompilerParams(vmem_limit_bytes=LIMIT << 20),
        name="conv_inner",
    )(weights, bias, coef, main, ylo, yhi)


def conv_outer(weights, bias, coef, state, faces, corners, volume):
    hbm = pl.BlockSpec(memory_space=pl.ANY)
    vmem = pl.BlockSpec(memory_space=pltpu.VMEM)
    return pl.pallas_call(
        outer_kernel,
        in_specs=[vmem] * 11 + [hbm],
        out_specs=hbm,
        scratch_shapes=[pltpu.VMEM((3 * C, WIDE), jnp.bfloat16)] * 4
        + [pltpu.VMEM((C * PITCH, Z), jnp.float32)] * 2
        + [
            pltpu.VMEM((4, C, BY, Z), jnp.bfloat16),
            pltpu.SemaphoreType.DMA((2, 2)),
        ],
        out_shape=jax.ShapeDtypeStruct((C, BX, BY, Z), jnp.bfloat16),
        input_output_aliases={11: 0},
        compiler_params=pltpu.CompilerParams(vmem_limit_bytes=LIMIT << 20),
        name="conv_outer",
    )(weights, bias, coef, *state, *faces, *corners, volume)


def shift(array, along_y, along_x):
    views, bricks = lax.axis_size("views"), lax.axis_size("bricks")
    pairs = [
        (v * bricks + b, (v + along_y) * bricks + b + along_x)
        for v in range(views)
        for b in range(bricks)
        if 0 <= v + along_y < views and 0 <= b + along_x < bricks
    ]
    return lax.ppermute(array, ("views", "bricks"), pairs)


def on_device(
    tile_pixel, tile_voxel, tile_count, features, interp, conv_weight, conv_bias, smooth_coef
):
    feats = features[0, 0]
    tiles = interp[0, 0]
    packed, weights, bias = partials(
        tile_pixel[0, 0],
        tile_voxel[0, 0],
        tile_count[0],
        feats,
        conv_weight.reshape(27, C, C),
        conv_bias[None],
        tiles,
    )
    got = lax.all_to_all(packed, ("views", "bricks"), split_axis=0, concat_axis=0, tiled=True)
    main, lo, hi, ylo, yhi = lift(got)
    from_low = shift(yhi, 1, 0)
    from_high = shift(ylo, -1, 0)
    faces = shift(hi, 0, 1), shift(lo, 0, -1)
    corners = (
        shift(jnp.stack([from_low[BX - 2 :], from_high[BX - 2 :]]), 0, 1),
        shift(jnp.stack([from_low[:2], from_high[:2]]), 0, -1),
    )
    volume, *state = conv_inner(weights, bias, smooth_coef, main, from_low, from_high)
    return conv_outer(weights, bias, smooth_coef, state, faces, corners, volume)


def solution(mesh):
    in_specs = (
        P("views", "bricks", None),
        P("views", "bricks", None),
        P("views", "bricks"),
        P("views", "bricks", None, None, None),
        P("views", "bricks", None, None, None),
        P(),
        P(),
        P("bricks", "views", None),
    )
    out_specs = P(None, "bricks", "views", None)
    return jax.shard_map(
        on_device, mesh=mesh, in_specs=in_specs, out_specs=out_specs, check_vma=False
    )
```
